128 devices in a mesh: lat: 8 (over y, core), lon: 16 (over x, z).
Axes of the slice: x: 4, y: 4, z: 4, core: 2. Of those that a mesh axis runs over, the one named last changes fastest.
Arguments:
- atmosphere: bfloat16 [2048, 1024, 256], P('lat', 'lon'), may hold values from -6 to 6
- dw_kernel: float32 [2, 16, 256], replicated, may hold values from -1.5 to 1.5
- norm_gain: float32 [2, 256], replicated, may hold values from 0.5 to 1.5
- w_in: bfloat16 [2, 256, 1024], replicated, may hold values from -0.375 to 0.375
- w_out: bfloat16 [2, 1024, 256], replicated, may hold values from -0.1875 to 0.1875
- w_flux: bfloat16 [256, 256], replicated, may hold values from -0.375 to 0.375
- remap_weight: bfloat16 [16384, 128, 128], P(('lat', 'lon')), may hold values from -0.5 to 0.5
- block_tile: int32 [16384], P(('lat', 'lon')), may hold values from 0 to 7
- block_owner: int32 [16384, 1], P(('lat', 'lon')), may hold values from 0 to 127; in each aligned block of 128 rows (0 to 127, 128 to 255, ...) at most 2 rows name the same one
- block_ocean: int32 [16384], P(('lat', 'lon')), may hold values from 0 to 15
Outputs:
- ocean_flux: float32 [262144, 256], P(('lat', 'lon'))
The draws below stay inside these ranges and needn't reach their ends.
Inputs may be any that keep to these rules, and one draw needn't show every extreme that they name: `block_owner`: the 128 blocks of one device name any one owner at most 2 times, and some device names some owner exactly 2 times.
All inputs are finite; a program needn't handle non-finite values.
Results may differ from the reference program's by a relative error of at most 0.02.
Values may be sent and summed in bfloat16 or wider, within the bound.
No kernel may reach another device: no remote copies, remote signals or barrier semaphores. Data moves between devices by JAX's collectives and lax.ppermute only.
A program may use at most 192 MiB of HBM per device.

```python
import math
import jax
import jax.numpy as jnp
import numpy as np
from jax import lax

C = 256
HID = 1024
LAYERS = 2
TILE = 128
OCELLS = 128
CAP = 2
OB_DEV = 16
BLOCKS_DEV = 128
TILES = 8
NLAT = 2048
NLON = 1024
ALL_BLOCKS = 16384
N_LAT = 8
N_LON = 16
DEVICES = 128


def touch_ends(array, own_key, smallest, largest):
    longest = array.shape.index(max(array.shape))
    spots = []
    for shift in (0, 1):
        where = [jax.random.randint(jax.random.fold_in(own_key, axis), (), 0, length) for axis, length in enumerate(array.shape)]
        where[longest] = (where[longest] + shift) % array.shape[longest]
        spots.append(tuple(where))
    return array.at[spots[0]].set(smallest).at[spots[1]].set(largest)


def block_levels(stream_key, extent, split, smallest, high):
    factor_of = 1.0
    for axis_at, parts in split:
        steps = jax.random.uniform(jax.random.fold_in(jax.random.fold_in(stream_key, 6), axis_at), (parts,), jnp.float32, smallest / len(split), high / len(split))
        factor_of = factor_of * jnp.repeat(jnp.exp(steps), extent[axis_at] // parts).reshape((-1,) + (1,) * (len(extent) - 1 - axis_at))
    return factor_of


def deal_out(rng, own, number, rows, number_of, top, limit, lean):
    order = jax.random.permutation(rng, number_of)
    crowded, usual = portions_of(number_of, rows * top, limit, lean, True), portions_of(number_of, rows * top, limit, lean, False)
    places = jnp.arange(number_of)

    def named(lengths, rotation):
        used = int((lengths > 0).sum())
        fixed = max(1, used // 4)
        shifted = fixed + (places - fixed + rotation * (used - fixed)) % max(1, number_of - fixed)
        return jnp.zeros((number_of,), jnp.int32).at[order[jnp.where(places < fixed, places, shifted)]].set(jnp.asarray(lengths, jnp.int32))

    lengths = jnp.where(number % 4 == 0, named(crowded, number // 4), named(usual, number - number // 4 - 1))
    mixed = jax.random.permutation(jax.random.fold_in(own, 3), number_of)
    giver, sink = mixed[0:number_of // 2 * 2:2], mixed[1:number_of // 2 * 2:2]
    slack = jnp.minimum(lengths[giver] - 1, limit - lengths[sink]) // 2
    slack = jnp.where((giver == order[0]) | (sink == order[0]) | (lengths[sink] == 0), 0, jnp.maximum(slack, 0))
    shifted = jax.random.randint(jax.random.fold_in(own, 4), (number_of // 2,), 0, 1 << 20) % (slack + 1)
    lengths = lengths.at[giver].add(-shifted).at[sink].add(shifted)
    items = jnp.searchsorted(jnp.cumsum(lengths), jnp.arange(rows * top), side="right").astype(jnp.int32)
    listing = items.reshape(top, rows).T
    listing = listing[jax.random.permutation(jax.random.fold_in(own, 1), rows)]
    rotation = jax.random.randint(jax.random.fold_in(own, 2), (rows, 1), 0, top)
    return jnp.take_along_axis(listing, (jnp.arange(top)[None, :] + rotation) % top, axis=1)


def portions_of(amount, total, bound, skew, full):
    loads = [(1 << 20) // math.isqrt(standing ** skew) + 1 for standing in range(1, amount + 1)]
    largest = bound if full else min(bound, max(-(-total // amount), total * loads[0] // sum(loads)))
    least = 1 if total - largest >= amount - 1 else 0
    given, spare = [largest] + [least] * (amount - 1), total - largest - least * (amount - 1)
    while spare > 0:
        free = [i for i in range(1, amount) if given[i] < largest] or [i for i in range(1, amount) if given[i] < bound]
        whole, remaining = sum([loads[i] for i in free]), spare
        for i in free:
            extra = min(bound - given[i], max(1, remaining * loads[i] // whole), spare)
            given[i] = given[i] + extra
            spare = spare - extra
    return np.array(given)


def noise(rng, extent, deviation, reach, cuts=(), kind=jnp.bfloat16):
    entries = deviation * jax.random.normal(rng, extent, jnp.float32)
    if cuts:
        entries = entries * block_levels(rng, extent, cuts, -0.22, 0.18)
    return jnp.clip(entries, -reach, reach).astype(kind)


def setup_inputs(seed: int = 0) -> dict:
    key_of = jax.random.split(jax.random.key(seed), 11)
    atmosphere = noise(key_of[0], (NLAT, NLON, C), 1.0, 6.0, ((0, 8), (1, 16)))
    dw_kernel = noise(key_of[1], (LAYERS, 16, C), 16 ** -0.5, 1.5, (), jnp.float32)
    norm_gain = jnp.clip(jax.random.uniform(key_of[2], (LAYERS, C), jnp.float32, 0.5, 1.5), 0.5, 1.5)
    w_in = noise(key_of[3], (LAYERS, C, HID), C ** -0.5, 0.375)
    w_out = noise(key_of[4], (LAYERS, HID, C), HID ** -0.5, 0.1875)
    w_flux = noise(key_of[5], (C, C), C ** -0.5, 0.375)
    remap_weight = noise(key_of[6], (ALL_BLOCKS, OCELLS, TILE), TILE ** -0.5, 0.5, ((0, 128),))
    block_tile = touch_ends(jax.random.randint(key_of[7], (ALL_BLOCKS,), 0, TILES), jax.random.fold_in(key_of[7], 1), 0, TILES - 1).astype(jnp.int32)
    block_owner_keys = jax.random.split(jax.random.fold_in(key_of[8], 1), ALL_BLOCKS // BLOCKS_DEV)
    block_owner_turns = jax.random.permutation(jax.random.fold_in(key_of[8], 3), ALL_BLOCKS // BLOCKS_DEV)
    block_owner = jax.vmap(lambda own, number: deal_out(jax.random.fold_in(key_of[8], 2), own, number, BLOCKS_DEV, DEVICES, 1, CAP, 2))(block_owner_keys, block_owner_turns).reshape((ALL_BLOCKS, 1))
    block_ocean = touch_ends(jax.random.randint(key_of[9], (ALL_BLOCKS,), 0, OB_DEV), jax.random.fold_in(key_of[9], 1), 0, OB_DEV - 1).astype(jnp.int32)
    return {"atmosphere": atmosphere, "dw_kernel": dw_kernel, "norm_gain": norm_gain, "w_in": w_in, "w_out": w_out, "w_flux": w_flux, "remap_weight": remap_weight, "block_tile": block_tile, "block_owner": block_owner, "block_ocean": block_ocean}


def rms_scale(values, gain_row):
    mean_sq = lax.optimization_barrier(jnp.mean(values * values, axis=-1, keepdims=True))
    return values * lax.rsqrt(mean_sq + 1e-06) * gain_row

def depthwise(padded, kernel, out_rows, out_cols):
    accum_sum = jnp.zeros((out_rows, out_cols, padded.shape[2]), jnp.float32)
    for tap_row in range(4):
        for tap_col in range(4):
            window = padded[tap_row:tap_row + 2 * out_rows - 1:2, tap_col:tap_col + 2 * out_cols - 1:2, :]
            accum_sum = accum_sum + window.astype(jnp.float32) * kernel[tap_row * 4 + tap_col]
    return accum_sum.astype(jnp.bfloat16)

def mix_channels(flat_cells, gain_row, w_in, w_out):
    normed = rms_scale(flat_cells.astype(jnp.float32), gain_row).astype(jnp.bfloat16)
    hidden = jax.nn.gelu(jnp.dot(normed, w_in, preferred_element_type=jnp.float32), approximate=True).astype(jnp.bfloat16)
    return (flat_cells.astype(jnp.float32) + jnp.dot(hidden, w_out, preferred_element_type=jnp.float32)).astype(jnp.bfloat16)

def encode_layer(current, kernel, gain_row, w_in, w_out):
    out_rows, out_cols = (current.shape[0] // 2, current.shape[1] // 2)
    padded = jnp.pad(current, ((1, 1), (0, 0), (0, 0)))
    padded = jnp.concatenate([padded[:, -1:], padded, padded[:, :1]], axis=1)
    depth_out = depthwise(padded, kernel, out_rows, out_cols)

    def one_row(row_cells):
        return mix_channels(row_cells, gain_row, w_in, w_out)
    return lax.map(one_row, depth_out)

def reference(atmosphere, dw_kernel, norm_gain, w_in, w_out, w_flux, remap_weight, block_tile, block_owner, block_ocean):
    current = atmosphere
    for section in range(LAYERS):
        current = encode_layer(current, dw_kernel[section], norm_gain[section], w_in[section], w_out[section])
    enc_lat = current.shape[0] // N_LAT
    enc_lon = current.shape[1] // N_LON
    surface_flux = jnp.dot(current.reshape(-1, C), w_flux, preferred_element_type=jnp.float32).astype(jnp.bfloat16)
    tile_rows = surface_flux.reshape(N_LAT, enc_lat, N_LON, enc_lon, C).transpose(0, 2, 1, 3, 4)
    tile_rows = tile_rows.reshape(N_LAT * N_LON, -1, TILE, C)
    weights = remap_weight.reshape(N_LAT * N_LON, BLOCKS_DEV, OCELLS, TILE)
    tile_index = block_tile.reshape(N_LAT * N_LON, BLOCKS_DEV)
    targets = (block_owner[:, 0] * OB_DEV + block_ocean).astype(jnp.int32).reshape(N_LAT * N_LON, BLOCKS_DEV)

    def one_device(ocean_sum, pieces):
        dev_tiles, dev_weights, dev_index, dev_targets = pieces
        chosen = dev_tiles[dev_index]
        contribs = jnp.einsum('bxt,btc->bxc', dev_weights.astype(jnp.float32), chosen.astype(jnp.float32)).astype(jnp.bfloat16)
        return (ocean_sum.at[dev_targets].add(contribs.astype(jnp.float32)), None)
    start = jnp.zeros((N_LAT * N_LON * OB_DEV, OCELLS, C), jnp.float32)
    ocean_sum, _ = lax.scan(one_device, start, (tile_rows, weights, tile_index, targets))
    return ocean_sum.reshape(-1, C)
```

```python
import functools
import jax
import jax.numpy as jnp
from jax import lax
from jax.experimental import pallas as pl
from jax.experimental.pallas import tpu as pltpu
from jax.sharding import PartitionSpec as P

CAP = 2
OB_DEV = 16
BOTH = ("lat", "lon")
PAD = 8


def shift(value, axis, periodic):
    count = lax.axis_size(axis)
    forward = [(i, i + 1) for i in range(count - 1)]
    if periodic:
        forward.append((count - 1, 0))
    backward = [(target, source) for source, target in forward]
    return (
        lax.ppermute(value[1], axis, forward),
        lax.ppermute(value[0], axis, backward),
    )


def layer_body(rows, cols, steps, with_flux, *refs):
    if with_flux:
        (x_ref, prev_ref, next_ref, top_ref, bot_ref, left_ref, right_ref, kern_ref, gain_ref,
         win_ref, wout_ref, wflux_ref, out_ref, xs, dep) = refs
    else:
        (x_ref, prev_ref, next_ref, top_ref, bot_ref, left_ref, right_ref, kern_ref, gain_ref,
         win_ref, wout_ref, out_ref, edge_ref, xs, dep) = refs
    step = pl.program_id(0)
    half = cols // 2

    def put(slot, value):
        value = value.astype(jnp.float32)
        xs[slot, 0, PAD:PAD + cols, :] = value[:, :128]
        xs[slot, 1, PAD:PAD + cols, :] = value[:, 128:]

    first = jnp.where(step == 0, top_ref[...].astype(jnp.float32), prev_ref[0].astype(jnp.float32))
    last = jnp.where(
        step == steps - 1, bot_ref[...].astype(jnp.float32), next_ref[0].astype(jnp.float32)
    )
    put(0, first)
    put(2 * rows + 1, last)
    for r in range(2 * rows):
        put(r + 1, x_ref[r])
    base = pl.multiple_of(step * (2 * rows), 2 * rows)
    near = left_ref[pl.ds(base, 2 * rows + 8), :]
    far = right_ref[pl.ds(base, 2 * rows + 8), :]
    for r in range(2 * rows + 2):
        for h in range(2):
            lanes = slice(128 * h, 128 * h + 128)
            xs[r, h, PAD - 1:PAD, :] = near[r:r + 1, lanes]
            xs[r, h, PAD + cols:PAD + cols + 1, :] = far[r:r + 1, lanes]
    for h in range(2):
        lanes = slice(128 * h, 128 * h + 128)
        for k in range(rows):
            total = jnp.zeros((half, 128), jnp.float32)
            for p in range(4):
                for q in range(4):
                    window = xs[2 * k + p, h, pl.ds(PAD - 1 + q, half, stride=2), :]
                    total = total + window * kern_ref[4 * p + q:4 * p + q + 1, lanes]
            dep[k * half:(k + 1) * half, lanes] = total
    flat = dep[...].astype(jnp.bfloat16).astype(jnp.float32)
    mean_sq = jnp.mean(flat * flat, axis=-1, keepdims=True)
    normed = (flat * lax.rsqrt(mean_sq + 1e-06) * gain_ref[...]).astype(jnp.bfloat16)
    wide = jnp.dot(normed, win_ref[...], preferred_element_type=jnp.float32)
    hidden = jax.nn.gelu(wide, approximate=True).astype(jnp.bfloat16)
    mixed = flat + jnp.dot(hidden, wout_ref[...], preferred_element_type=jnp.float32)
    if with_flux:
        out_ref[...] = jnp.dot(
            mixed.astype(jnp.bfloat16), wflux_ref[...], preferred_element_type=jnp.float32
        ).astype(jnp.bfloat16)
    else:
        out_ref[...] = mixed.astype(jnp.bfloat16).reshape(rows, half, mixed.shape[1])


def encode_layer(current, layer, dw_kernel, norm_gain, w_in, w_out, w_flux, rows):
    in_rows, in_cols, channels = current.shape
    out_rows, out_cols = in_rows // 2, in_cols // 2
    hid = w_in.shape[2]
    steps = out_rows // rows
    top, bot = shift((current[:1], current[-1:]), "lat", False)
    sides = [
        jnp.concatenate([top[:, c], current[:, c], bot[:, c]], axis=0) for c in (0, in_cols - 1)
    ]
    left, right = shift(sides, "lon", True)
    left = jnp.pad(left.astype(jnp.float32), ((0, 6), (0, 0)))
    right = jnp.pad(right.astype(jnp.float32), ((0, 6), (0, 0)))
    with_flux = w_flux is not None
    whole = lambda shape: pl.BlockSpec(shape, lambda i: (0,) * len(shape))
    pick = lambda shape: pl.BlockSpec((None,) + shape, lambda i: (layer,) + (0,) * len(shape))
    in_specs = [
        pl.BlockSpec((2 * rows, in_cols, channels), lambda i: (i, 0, 0)),
        pl.BlockSpec((1, in_cols, channels), lambda i: (jnp.maximum(2 * rows * i - 1, 0), 0, 0)),
        pl.BlockSpec(
            (1, in_cols, channels), lambda i: (jnp.minimum(2 * rows * (i + 1), in_rows - 1), 0, 0)
        ),
        whole((in_cols, channels)),
        whole((in_cols, channels)),
        whole((in_rows + 8, channels)),
        whole((in_rows + 8, channels)),
        pick((16, channels)),
        pick((1, channels)),
        pick((channels, hid)),
        pick((hid, channels)),
    ]
    operands = [current, current, current, top[0], bot[0], left, right, dw_kernel,
                norm_gain[:, None, :], w_in, w_out]
    cells = out_rows * out_cols
    if with_flux:
        in_specs.append(whole((channels, channels)))
        operands.append(w_flux)
        out_specs = pl.BlockSpec((rows * out_cols, channels), lambda i: (i, 0))
        out_shape = jax.ShapeDtypeStruct((cells, channels), jnp.bfloat16)
    else:
        out_specs = pl.BlockSpec((rows, out_cols, channels), lambda i: (i, 0, 0))
        out_shape = jax.ShapeDtypeStruct((out_rows, out_cols, channels), jnp.bfloat16)

    def body(*refs):
        if with_flux:
            layer_body(rows, in_cols, steps, True, *refs)
        else:
            layer_body(rows, in_cols, steps, False, *refs[:12], None, *refs[12:])

    return pl.pallas_call(
        body,
        grid=(steps,),
        in_specs=in_specs,
        out_specs=out_specs,
        out_shape=out_shape,
        scratch_shapes=[
            pltpu.VMEM((2 * rows + 2, 2, in_cols + 2 * PAD, 128), jnp.float32),
            pltpu.VMEM((rows * out_cols, channels), jnp.float32),
        ],
        compiler_params=pltpu.CompilerParams(vmem_limit_bytes=48 << 20),
        name="layer",
    )(*operands)


def index(shape, dim):
    return lax.broadcasted_iota(jnp.int32, shape, dim)


def matmul(lhs, rhs, rhs_dim):
    return lax.dot_general(
        lhs.astype(jnp.float32), rhs.astype(jnp.float32), (((1,), (rhs_dim,)), ((), ())),
        preferred_element_type=jnp.float32,
    )


def route_body(owner_row_ref, owner_ref, ocean_ref, tile_ref, out_ref):
    owner = owner_ref[...]
    blocks = owner.shape[0]
    square = (blocks, blocks)
    same = (owner == owner_row_ref[...]) & (index(square, 1) < index(square, 0))
    rank = jnp.sum(same.astype(jnp.int32), axis=1, keepdims=True)
    mine = owner == index(square, 1)
    out_ref[...] = jnp.zeros_like(out_ref)
    for r in range(CAP):
        hit = (mine & (rank == r)).astype(jnp.int32)
        sums = lambda column: jnp.sum(hit * column, axis=0, keepdims=True)
        out_ref[r:r + 1, :] = sums(ocean_ref[...] + 1) - 1
        out_ref[2 + r:3 + r, :] = sums(index((blocks, 1), 0))
        out_ref[4 + r:5 + r, :] = sums(tile_ref[...])


def route(owner, ocean, tile):
    blocks = owner.shape[0]
    return pl.pallas_call(
        route_body,
        out_shape=jax.ShapeDtypeStruct((32, blocks), jnp.int32),
        name="route",
    )(owner.reshape(1, blocks), owner, ocean.reshape(blocks, 1), tile.reshape(blocks, 1))


def plan_body(me_ref, table_ref, own_ref, row_ref, bins_ref):
    devices = table_ref.shape[0]
    square = (devices, devices)
    spare = table_ref[:, 1, :]
    hot = jnp.max(spare, axis=0, keepdims=True) >= 0
    hot8 = jnp.broadcast_to(hot, (8, devices)).astype(jnp.float32)
    before = (index(square, 0) < index(square, 1)).astype(jnp.float32)
    rank = matmul(hot8, before, 0).astype(jnp.int32)
    listed = (jnp.broadcast_to(hot, square) & (rank[:1] == index(square, 0))).astype(jnp.float32)
    bins_ref[...] = matmul(listed, spare + 1, 1).astype(jnp.int32) - 1
    me = (index((8, devices), 1) == me_ref[0]).astype(jnp.float32)
    row_ref[0:8] = matmul(me, table_ref[:, 0, :] + 1, 1).astype(jnp.int32) - 1
    own = own_ref[...]
    row_ref[8:16] = matmul(own[0:8], listed, 1).astype(jnp.int32)
    row_ref[16:24] = jnp.where(hot8 > 0, rank, -1)
    row_ref[24:32] = jnp.broadcast_to(
        jnp.sum(hot8, axis=1, keepdims=True).astype(jnp.int32), (8, devices)
    )


def plan(me, table, own):
    devices = table.shape[0]
    grid_spec = pltpu.PrefetchScalarGridSpec(
        num_scalar_prefetch=1,
        grid=(1,),
        in_specs=[
            pl.BlockSpec((devices, 8, devices), lambda i, *_: (0, 0, 0)),
            pl.BlockSpec((8, devices), lambda i, *_: (0, 0)),
        ],
        out_specs=[
            pl.BlockSpec((32, devices), lambda i, *_: (0, 0)),
            pl.BlockSpec((devices, devices), lambda i, *_: (0, 0)),
        ],
    )
    return pl.pallas_call(
        plan_body,
        grid_spec=grid_spec,
        out_shape=[
            jax.ShapeDtypeStruct((32, devices), jnp.int32),
            jax.ShapeDtypeStruct((devices, devices), jnp.int32),
        ],
        name="plan",
    )(me.reshape(1), table, own)


def remap_body(group, item_ref, tile_ref, w_ref, flux_ref, out_ref):
    base = pl.program_id(0) * group
    for j in range(group):
        out_ref[j] = jnp.dot(
            w_ref[item_ref[base + j]], flux_ref[tile_ref[base + j]],
            preferred_element_type=jnp.float32,
        ).astype(jnp.bfloat16)


def remap(items, tiles, weights, flux, group):
    slots = items.shape[0]
    _, cells, tile = weights.shape
    channels = flux.shape[2]
    grid_spec = pltpu.PrefetchScalarGridSpec(
        num_scalar_prefetch=2,
        grid=(slots // group,),
        in_specs=[
            pl.BlockSpec(weights.shape, lambda i, *_: (0, 0, 0)),
            pl.BlockSpec(flux.shape, lambda i, *_: (0, 0, 0)),
        ],
        out_specs=pl.BlockSpec((group, cells, channels), lambda i, *_: (i, 0, 0)),
    )
    return pl.pallas_call(
        functools.partial(remap_body, group),
        grid_spec=grid_spec,
        out_shape=jax.ShapeDtypeStruct((slots, cells, channels), jnp.bfloat16),
        compiler_params=pltpu.CompilerParams(vmem_limit_bytes=48 << 20),
        name="remap",
    )(items, tiles, weights, flux)


def remap_spare_body(parts, item_ref, tile_ref, w_ref, flux_ref, out_ref):
    rows = out_ref.shape[2]
    for h in range(out_ref.shape[1]):
        block = jnp.dot(
            w_ref[item_ref[h]], flux_ref[tile_ref[h]], preferred_element_type=jnp.float32
        ).astype(jnp.bfloat16)
        for p in range(parts):
            out_ref[p, h] = block[p * rows:(p + 1) * rows]


def remap_spare(items, tiles, weights, flux, parts):
    slots = items.shape[0]
    _, cells, tile = weights.shape
    channels = flux.shape[2]
    out = (parts, slots, cells // parts, channels)
    grid_spec = pltpu.PrefetchScalarGridSpec(
        num_scalar_prefetch=2,
        grid=(1,),
        in_specs=[
            pl.BlockSpec(weights.shape, lambda i, *_: (0, 0, 0)),
            pl.BlockSpec(flux.shape, lambda i, *_: (0, 0, 0)),
        ],
        out_specs=pl.BlockSpec(out, lambda i, *_: (0, 0, 0, 0)),
    )
    return pl.pallas_call(
        functools.partial(remap_spare_body, parts),
        grid_spec=grid_spec,
        out_shape=jax.ShapeDtypeStruct(out, jnp.bfloat16),
        compiler_params=pltpu.CompilerParams(vmem_limit_bytes=48 << 20),
        name="remap_spare",
    )(items, tiles, weights, flux)


def part_sum_body(bin_ref, x_ref, out_ref, acc):
    acc[...] = jnp.zeros_like(acc)

    def add(s, carry):
        spot = bin_ref[s]

        @pl.when(spot >= 0)
        def _():
            acc[spot] += x_ref[s].astype(jnp.float32)

        return carry

    lax.fori_loop(0, x_ref.shape[0], add, 0)
    out_ref[...] = acc[...].astype(jnp.bfloat16)


def part_sum(bins, arrived):
    sources, rows, channels = arrived.shape
    out = (OB_DEV, rows, channels)
    return pl.pallas_call(
        part_sum_body,
        in_specs=[
            pl.BlockSpec(memory_space=pltpu.SMEM),
            pl.BlockSpec(memory_space=pltpu.VMEM),
        ],
        out_specs=pl.BlockSpec(memory_space=pltpu.VMEM),
        out_shape=jax.ShapeDtypeStruct(out, jnp.bfloat16),
        scratch_shapes=[pltpu.VMEM(out, jnp.float32)],
        compiler_params=pltpu.CompilerParams(vmem_limit_bytes=32 << 20),
        name="part_sum",
    )(bins, arrived)


def pick_body(spot_ref, x_ref, *out_refs):
    for k, out_ref in enumerate(out_refs):
        out_ref[...] = x_ref[spot_ref[k]]


def pick(spots, gathered, count):
    piece = gathered.shape[1:]
    return pl.pallas_call(
        pick_body,
        in_specs=[
            pl.BlockSpec(memory_space=pltpu.SMEM),
            pl.BlockSpec(memory_space=pltpu.VMEM),
        ],
        out_specs=[pl.BlockSpec(memory_space=pltpu.VMEM)] * count,
        out_shape=[jax.ShapeDtypeStruct(piece, jnp.bfloat16)] * count,
        compiler_params=pltpu.CompilerParams(vmem_limit_bytes=32 << 20),
        name="pick",
    )(spots, gathered)


def add_parts(info_ref, part_refs, out_ref):
    count = len(part_refs)
    rows = part_refs[0].shape[1]

    @pl.when(info_ref[0] > 0)
    def _():
        for k, part_ref in enumerate(part_refs):
            part = lax.rem(info_ref[1] + (count - k), count)
            start = pl.multiple_of(part * rows, rows)
            out_ref[:, pl.ds(start, rows), :] += part_ref[...].astype(jnp.float32)


def owner_body(group, steps, bin_ref, info_ref, x_ref, *refs):
    part_refs, out_ref = refs[:-1], refs[-1]
    step = pl.program_id(0)

    @pl.when(step == 0)
    def _():
        out_ref[...] = jnp.zeros_like(out_ref)

    for j in range(group):
        spot = bin_ref[step * group + j]

        @pl.when(spot >= 0)
        def _():
            out_ref[spot] += x_ref[j].astype(jnp.float32)

    @pl.when(step == steps - 1)
    def _():
        add_parts(info_ref, part_refs, out_ref)


def owner_sum(bins, info, arrived, parts, group):
    slots, cells, channels = arrived.shape
    steps = slots // group
    whole = lambda i, *_: (0, 0, 0)
    grid_spec = pltpu.PrefetchScalarGridSpec(
        num_scalar_prefetch=2,
        grid=(steps,),
        in_specs=[pl.BlockSpec((group, cells, channels), lambda i, *_: (i, 0, 0))]
        + [pl.BlockSpec(part.shape, whole) for part in parts],
        out_specs=pl.BlockSpec((OB_DEV, cells, channels), whole),
    )
    return pl.pallas_call(
        functools.partial(owner_body, group, steps),
        grid_spec=grid_spec,
        out_shape=jax.ShapeDtypeStruct((OB_DEV, cells, channels), jnp.float32),
        compiler_params=pltpu.CompilerParams(vmem_limit_bytes=48 << 20),
        name="owner_sum",
    )(bins, info, arrived, *parts)


def late_body(info_ref, total_ref, *refs):
    part_refs, out_ref = refs[:-1], refs[-1]
    out_ref[...] = total_ref[...]
    add_parts(info_ref, part_refs, out_ref)


def late_sum(info, total, parts):
    vmem = pl.BlockSpec(memory_space=pltpu.VMEM)
    return pl.pallas_call(
        late_body,
        in_specs=[pl.BlockSpec(memory_space=pltpu.SMEM), vmem] + [vmem] * len(parts),
        out_specs=vmem,
        out_shape=jax.ShapeDtypeStruct(total.shape, jnp.float32),
        compiler_params=pltpu.CompilerParams(vmem_limit_bytes=32 << 20),
        name="late_sum",
    )(info, total, *parts)


def spare_round(turn, rows, bins, weights, flux, make_main):
    lats, lons = lax.axis_size("lat"), lax.axis_size("lon")
    lat, lon = lax.axis_index("lat"), lax.axis_index("lon")
    first = turn * lons
    window = lambda row: lax.dynamic_slice_in_dim(rows[row], first, lons)
    sending = remap_spare(window(10 + 1), window(12 + 1), weights, flux, lats)
    sending = sending.reshape((lats * lons,) + sending.shape[2:])
    arrived = lax.all_to_all(sending, BOTH, split_axis=0, concat_axis=0, tiled=True)
    main = None
    if make_main is not None:
        main, arrived = make_main(arrived)
    my_bins = lax.dynamic_index_in_dim(bins, first + lon, axis=0, keepdims=False)
    part = part_sum(my_bins, arrived)
    gathered = lax.all_gather(part, "lon", axis=0, tiled=False)
    ranks = rows[16].reshape(lats, lons)
    column = lax.dynamic_index_in_dim(ranks, lon, axis=1, keepdims=False) - first
    here = (column >= 0) & (column < lons)
    turned = jnp.roll(jnp.where(here, column, 0), -lat)
    picked = pick(turned, gathered, lats)
    parts = [picked[0]]
    for k in range(1, lats):
        parts.append(lax.ppermute(picked[k], "lat", [(i, (i + k) % lats) for i in range(lats)]))
    mine = lax.dynamic_index_in_dim(here, lat, axis=0, keepdims=False).astype(jnp.int32)
    return main, jnp.stack([mine, lat.astype(jnp.int32)]), parts


def shards(atmosphere, dw_kernel, norm_gain, w_in, w_out, w_flux, remap_weight, block_tile,
           block_owner, block_ocean):
    lons = lax.axis_size("lon")
    own = route(block_owner, block_ocean, block_tile)
    table = lax.all_gather(own, BOTH, axis=0, tiled=False)
    hidden = encode_layer(atmosphere, 0, dw_kernel, norm_gain, w_in, w_out, None, 8)
    rows, bins = plan(lax.axis_index(BOTH), table, own)
    flux = encode_layer(hidden, 1, dw_kernel, norm_gain, w_in, w_out, w_flux, 16)
    channels = flux.shape[1]
    flux = flux.reshape(-1, remap_weight.shape[2], channels)

    def make_main(early):
        sending = remap(own[2], own[4], remap_weight, flux, 16)
        sending, early = lax.optimization_barrier((sending, early))
        return lax.all_to_all(sending, BOTH, split_axis=0, concat_axis=0, tiled=True), early

    main, info, parts = spare_round(0, rows, bins, remap_weight, flux, make_main)
    total = owner_sum(rows[0], info, main, parts, 16)

    def more(state):
        turn, _ = state
        return turn * lons < rows[24, 0]

    def again(state):
        turn, total = state
        _, info, parts = spare_round(turn, rows, bins, remap_weight, flux, None)
        return turn + 1, late_sum(info, total, parts)

    _, total = lax.while_loop(more, again, (jnp.int32(1), total))
    return total.reshape(-1, channels)


def solution(mesh):
    placed = (
        P("lat", "lon", None),
        P(),
        P(),
        P(),
        P(),
        P(),
        P(BOTH, None, None),
        P(BOTH),
        P(BOTH, None),
        P(BOTH),
    )
    return jax.shard_map(
        shards, mesh=mesh, in_specs=placed, out_specs=P(BOTH, None), check_vma=False
    )
```

```python
import functools
import jax
import jax.numpy as jnp
from jax import lax
from jax.experimental import pallas as pl
from jax.experimental.pallas import tpu as pltpu
from jax.sharding import PartitionSpec as P

CAP = 2
OB_DEV = 16
OWNERS = 16


def far(value):
    return pltpu.with_memory_space_constraint(value, pltpu.HBM)

BOTH = ("lat", "lon")
PAD = 8
GELU_A = 0.7978845608028654
GELU_B = 0.044715 * GELU_A


def shift(value, axis, periodic):
    count = lax.axis_size(axis)
    forward = [(i, i + 1) for i in range(count - 1)]
    if periodic:
        forward.append((count - 1, 0))
    backward = [(target, source) for source, target in forward]
    return (
        lax.ppermute(value[1], axis, forward),
        lax.ppermute(value[0], axis, backward),
    )


def mix(depth, gain_ref, win_ref, wout_ref):
    flat = depth.astype(jnp.bfloat16).astype(jnp.float32)
    mean_sq = jnp.mean(flat * flat, axis=-1, keepdims=True)
    normed = (flat * lax.rsqrt(mean_sq + 1e-06) * gain_ref[...]).astype(jnp.bfloat16)
    wide = jnp.dot(normed, win_ref[...], preferred_element_type=jnp.float32)
    inner = wide * (GELU_A + GELU_B * (wide * wide))
    hidden = (wide * (0.5 + 0.5 * jnp.tanh(inner))).astype(jnp.bfloat16)
    return flat + jnp.dot(hidden, wout_ref[...], preferred_element_type=jnp.float32)


def layer_body(rows, cols, steps, with_flux, *refs):
    if with_flux:
        (x_ref, prev_ref, next_ref, top_ref, bot_ref, left_ref, right_ref, kern_ref, gain_ref,
         win_ref, wout_ref, wflux_ref, out_ref, xs, dep) = refs
    else:
        (x_ref, prev_ref, next_ref, top_ref, bot_ref, left_ref, right_ref, kern_ref, gain_ref,
         win_ref, wout_ref, out_ref, edge_ref, xs, dep) = refs
    step = pl.program_id(0)
    half = cols // 2

    def put(slot, value):
        value = value.astype(jnp.float32)
        xs[slot, 0, PAD:PAD + cols, :] = value[:, :128]
        xs[slot, 1, PAD:PAD + cols, :] = value[:, 128:]

    first = jnp.where(step == 0, top_ref[...].astype(jnp.float32), prev_ref[0].astype(jnp.float32))
    last = jnp.where(
        step == steps - 1, bot_ref[...].astype(jnp.float32), next_ref[0].astype(jnp.float32)
    )
    put(0, first)
    put(2 * rows + 1, last)
    for r in range(2 * rows):
        put(r + 1, x_ref[r])
    base = pl.multiple_of(step * (2 * rows), 2 * rows)
    near = left_ref[pl.ds(base, 2 * rows + 8), :]
    after = right_ref[pl.ds(base, 2 * rows + 8), :]
    for r in range(2 * rows + 2):
        for h in range(2):
            lanes = slice(128 * h, 128 * h + 128)
            xs[r, h, PAD - 1:PAD, :] = near[r:r + 1, lanes]
            xs[r, h, PAD + cols:PAD + cols + 1, :] = after[r:r + 1, lanes]
    for h in range(2):
        lanes = slice(128 * h, 128 * h + 128)
        for k in range(rows):
            total = jnp.zeros((half, 128), jnp.float32)
            for p in range(4):
                for q in range(4):
                    window = xs[2 * k + p, h, pl.ds(PAD - 1 + q, half, stride=2), :]
                    total = total + window * kern_ref[4 * p + q:4 * p + q + 1, lanes]
            dep[k * half:(k + 1) * half, lanes] = total
    mixed = mix(dep[...], gain_ref, win_ref, wout_ref)
    if with_flux:
        out_ref[...] = jnp.dot(
            mixed.astype(jnp.bfloat16), wflux_ref[...], preferred_element_type=jnp.float32
        ).astype(jnp.bfloat16)
    else:
        out_ref[...] = mixed.astype(jnp.bfloat16).reshape(rows, half, mixed.shape[1])


def rim_body(edge_ref, from_left, from_right, left_ref, right_ref, top_ref, bot_ref, first_ref,
             last_ref, kern_ref, gain_ref, win_ref, wout_ref, left1, right1, left2, right2, top2,
             bot2, tall, wide, cells):
    rows = left_ref.shape[1] - 16
    cols = first_ref.shape[1]
    half_cols = cols // 2
    side = left2.shape[0]
    halves = [(h, slice(128 * h, 128 * h + 128)) for h in range(2)]
    strips = [(from_left, c) for c in range(3)] + [(left_ref, 0)]
    strips += [(right_ref, 2)] + [(from_right, c) for c in range(3)]
    for n, (ref, c) in enumerate(strips):
        value = ref[c].astype(jnp.float32)
        for h, lanes in halves:
            tall[n, h, PAD:PAD + rows, :] = value[:rows, lanes]
            tall[n, h, PAD - 3:PAD, :] = value[rows:rows + 3, lanes]
            tall[n, h, PAD + rows:PAD + rows + 3, :] = value[rows + 3:rows + 6, lanes]
            tall[n, h, PAD + rows + 3:, :] = jnp.zeros(
                (tall.shape[2] - PAD - rows - 3, 128), jnp.float32
            )
    for h, lanes in halves:
        left1[:, lanes] = tall[2, h, PAD - 1:PAD - 1 + left1.shape[0], :]
        right1[:, lanes] = tall[5, h, PAD - 1:PAD - 1 + right1.shape[0], :]
    lines = [(top_ref[i], i - 3) for i in range(3)] + [(first_ref[0], 0)]
    lines += [(last_ref[0], rows - 1)] + [(bot_ref[i], rows + i) for i in range(3)]
    for n, (value, row) in enumerate(lines):
        value = value.astype(jnp.float32)
        at = PAD + row
        for h, lanes in halves:
            wide[n, h, PAD:PAD + cols, :] = value[:, lanes]
            wide[n, h, PAD - 1:PAD, :] = tall[2, h, at:at + 1, :]
            wide[n, h, PAD + cols:PAD + cols + 1, :] = tall[5, h, at:at + 1, :]
    for h, lanes in halves:
        for part in range(2):
            total = jnp.zeros((side, 128), jnp.float32)
            line = jnp.zeros((half_cols, 128), jnp.float32)
            for p in range(4):
                for q in range(4):
                    tap = kern_ref[4 * p + q:4 * p + q + 1, lanes]
                    total = total + tall[4 * part + q, h, pl.ds(PAD - 3 + p, side, stride=2), :] * tap
                    line = line + wide[4 * part + p, h, pl.ds(PAD - 1 + q, half_cols, stride=2), :] * tap
            cells[side * part:side * part + side, lanes] = total
            at = 2 * side + half_cols * part
            cells[at:at + half_cols, lanes] = line
    mixed = mix(cells[...], gain_ref, win_ref, wout_ref).astype(jnp.bfloat16).astype(jnp.float32)
    place = index((side, mixed.shape[1]), 0)
    outside = ((place == 0) & (edge_ref[0] > 0)) | ((place == rows // 2 + 1) & (edge_ref[1] > 0))
    left2[...] = jnp.where(outside, 0.0, mixed[:side])
    right2[...] = jnp.where(outside, 0.0, mixed[side:2 * side])
    at = 2 * side
    top2[...] = jnp.where(edge_ref[0] > 0, 0.0, mixed[at:at + half_cols]).astype(jnp.bfloat16)
    bot2[...] = jnp.where(edge_ref[1] > 0, 0.0, mixed[at + half_cols:]).astype(jnp.bfloat16)


def rims(current, dw_kernel, norm_gain, w_in, w_out):
    rows, cols, channels = current.shape
    hid = w_in.shape[2]
    top, bot = shift((current[:3], current[-3:]), "lat", False)
    fill = jnp.zeros((3, 10, channels), current.dtype)
    sides = [
        jnp.concatenate(
            [jnp.swapaxes(part[:, c:c + 3], 0, 1) for part in (current, top, bot)] + [fill], axis=1
        )
        for c in (0, cols - 3)
    ]
    from_left, from_right = shift(sides, "lon", True)
    lat = lax.axis_index("lat")
    edge = jnp.stack([lat == 0, lat == lax.axis_size("lat") - 1]).astype(jnp.int32)
    whole = lambda shape: pl.BlockSpec(shape, lambda i: (0,) * len(shape))
    pick = lambda shape: pl.BlockSpec((None,) + shape, lambda i: (0,) * (len(shape) + 1))
    side = rows // 2 + 8
    outs = [(rows + 8, jnp.float32)] * 2 + [(side, jnp.float32)] * 2 + [(cols // 2, jnp.bfloat16)] * 2
    left1, right1, left2, right2, top2, bot2 = pl.pallas_call(
        rim_body,
        grid=(1,),
        in_specs=[pl.BlockSpec(memory_space=pltpu.SMEM)]
        + [whole(sides[0].shape)] * 4
        + [whole(top.shape)] * 2
        + [
            pl.BlockSpec((1, cols, channels), lambda i: (0, 0, 0)),
            pl.BlockSpec((1, cols, channels), lambda i: (rows - 1, 0, 0)),
            pick((16, channels)),
            pick((1, channels)),
            pick((channels, hid)),
            pick((hid, channels)),
        ],
        out_specs=[whole((count, channels)) for count, _ in outs],
        out_shape=[jax.ShapeDtypeStruct((count, channels), kind) for count, kind in outs],
        scratch_shapes=[
            pltpu.VMEM((8, 2, rows + 4 * PAD, 128), jnp.float32),
            pltpu.VMEM((8, 2, cols + 2 * PAD, 128), jnp.float32),
            pltpu.VMEM((2 * side + cols, channels), jnp.float32),
        ],
        compiler_params=pltpu.CompilerParams(vmem_limit_bytes=20 << 20),
        name="rim",
    )(edge, from_left, from_right, *sides, top, bot, far(current), far(current), dw_kernel,
      norm_gain[:, None, :], far(w_in), far(w_out))
    return (top[-1], bot[0], left1, right1), (top2, bot2, left2, right2)


def run_layer(current, halo, layer, dw_kernel, norm_gain, w_in, w_out, w_flux, rows):
    in_rows, in_cols, channels = current.shape
    out_rows, out_cols = in_rows // 2, in_cols // 2
    hid = w_in.shape[2]
    steps = out_rows // rows
    with_flux = w_flux is not None
    whole = lambda shape: pl.BlockSpec(shape, lambda i: (0,) * len(shape))
    pick = lambda shape: pl.BlockSpec((None,) + shape, lambda i: (layer,) + (0,) * len(shape))
    in_specs = [
        pl.BlockSpec((2 * rows, in_cols, channels), lambda i: (i, 0, 0)),
        pl.BlockSpec((1, in_cols, channels), lambda i: (jnp.maximum(2 * rows * i - 1, 0), 0, 0)),
        pl.BlockSpec(
            (1, in_cols, channels), lambda i: (jnp.minimum(2 * rows * (i + 1), in_rows - 1), 0, 0)
        ),
        whole((in_cols, channels)),
        whole((in_cols, channels)),
        whole((in_rows + 8, channels)),
        whole((in_rows + 8, channels)),
        pick((16, channels)),
        pick((1, channels)),
        pick((channels, hid)),
        pick((hid, channels)),
    ]
    field = current if with_flux else far(current)
    operands = [field, field, field, *halo, dw_kernel, norm_gain[:, None, :], far(w_in), far(w_out)]
    cells = out_rows * out_cols
    if with_flux:
        in_specs.append(whole((channels, channels)))
        operands.append(w_flux)
        out_specs = pl.BlockSpec((rows * out_cols, channels), lambda i: (i, 0))
        out_shape = jax.ShapeDtypeStruct((cells, channels), jnp.bfloat16)
    else:
        out_specs = pl.BlockSpec((rows, out_cols, channels), lambda i: (i, 0, 0))
        out_shape = jax.ShapeDtypeStruct((out_rows, out_cols, channels), jnp.bfloat16)

    def body(*refs):
        if with_flux:
            layer_body(rows, in_cols, steps, True, *refs)
        else:
            layer_body(rows, in_cols, steps, False, *refs[:12], None, *refs[12:])

    return pl.pallas_call(
        body,
        grid=(steps,),
        in_specs=in_specs,
        out_specs=out_specs,
        out_shape=out_shape,
        scratch_shapes=[
            pltpu.VMEM((2 * rows + 2, 2, in_cols + 2 * PAD, 128), jnp.float32),
            pltpu.VMEM((rows * out_cols, channels), jnp.float32),
        ],
        compiler_params=pltpu.CompilerParams(vmem_limit_bytes=28 << 20),
        cost_estimate=pl.CostEstimate(
            flops=cells * channels * hid // 4, transcendentals=0,
            bytes_accessed=2 * (in_rows * in_cols + cells) * channels,
        ),
        name="layer",
    )(*operands)


def index(shape, dim):
    return lax.broadcasted_iota(jnp.int32, shape, dim)


def matmul(lhs, rhs, rhs_dim):
    return lax.dot_general(
        lhs.astype(jnp.float32), rhs.astype(jnp.float32), (((1,), (rhs_dim,)), ((), ())),
        preferred_element_type=jnp.float32,
    )


def column_of(row):
    size = row.shape[1]
    square = (size, size)
    diagonal = index(square, 0) == index(square, 1)
    return jnp.sum(jnp.where(diagonal, jnp.broadcast_to(row, square), 0), axis=1, keepdims=True)


def route_body(owner_ref, ocean_ref, tile_ref, out_ref, code_ref):
    owner_row = owner_ref[...]
    blocks = owner_row.shape[1]
    owner, ocean, tile = (column_of(ref[...]) for ref in (owner_ref, ocean_ref, tile_ref))
    square = (blocks, blocks)
    same = (owner == owner_row) & (index(square, 1) < index(square, 0))
    rank = jnp.sum(same.astype(jnp.int32), axis=1, keepdims=True)
    mine = owner == index(square, 1)
    code = jnp.zeros((1, blocks), jnp.int32)
    for r in range(CAP):
        hit = (mine & (rank == r)).astype(jnp.int32)
        sums = lambda column: jnp.sum(hit * column, axis=0, keepdims=True)
        code = code * 32 + sums(ocean + 1)
        out_ref[r:r + 1, :] = sums(index((blocks, 1), 0))
        out_ref[2 + r:3 + r, :] = sums(tile)
    out_ref[4:8, :] = jnp.zeros((4, blocks), jnp.int32)
    code_ref[...] = jnp.broadcast_to(code, code_ref.shape)


def route(owner, ocean, tile):
    blocks = owner.shape[0]
    return pl.pallas_call(
        route_body,
        out_shape=[
            jax.ShapeDtypeStruct((8, blocks), jnp.int32),
            jax.ShapeDtypeStruct((blocks, blocks), jnp.int32),
        ],
        name="route",
    )(owner.reshape(1, blocks), ocean.reshape(1, blocks), tile.reshape(1, blocks))


def plan_body(me_ref, table_ref, own_ref, row_ref, bins_ref):
    code = table_ref[...]
    devices = code.shape[0]
    square = (devices, devices)
    spare = code & 31
    hot = jnp.max(spare, axis=0, keepdims=True) > 0
    hot8 = jnp.broadcast_to(hot, (8, devices)).astype(jnp.float32)
    before = (index(square, 0) < index(square, 1)).astype(jnp.float32)
    rank = matmul(hot8, before, 0).astype(jnp.int32)
    listed = (jnp.broadcast_to(hot, square) & (rank[:1] == index(square, 0))).astype(jnp.float32)
    bins_ref[...] = matmul(listed, spare, 1).astype(jnp.int32) - 1
    me = (index((8, devices), 1) == me_ref[0]).astype(jnp.float32)
    row_ref[0:8] = matmul(me, code >> 5, 1).astype(jnp.int32) - 1
    row_ref[8:16] = matmul(own_ref[...], listed, 1).astype(jnp.int32)
    row_ref[16:24] = jnp.where(hot8 > 0, rank, -1)
    row_ref[24:32] = jnp.broadcast_to(
        jnp.sum(hot8, axis=1, keepdims=True).astype(jnp.int32), (8, devices)
    )


def plan(me, table, own):
    devices = table.shape[0]
    vmem = pl.BlockSpec(memory_space=pltpu.VMEM)
    return pl.pallas_call(
        plan_body,
        in_specs=[pl.BlockSpec(memory_space=pltpu.SMEM), vmem, vmem],
        out_specs=[vmem, vmem],
        out_shape=[
            jax.ShapeDtypeStruct((32, devices), jnp.int32),
            jax.ShapeDtypeStruct((devices, devices), jnp.int32),
        ],
        name="plan",
    )(me.reshape(1), table, own)


def remap_body(group, main, item_ref, tile_ref, w_ref, flux_ref, out_ref, spare):
    step = pl.program_id(0)
    cells = w_ref.shape[1]

    def block(slot):
        return jnp.dot(
            w_ref[item_ref[slot]], flux_ref[tile_ref[slot]], preferred_element_type=jnp.float32
        )

    @pl.when(step == 0)
    def _():
        for h in range(OWNERS):
            rows = slice(h * cells, h * cells + cells)
            value = block(h)
            spare[0, rows, :] = value[:, :128]
            spare[1, rows, :] = value[:, 128:]

    for j in range(group):
        device = step * group + j
        if main:
            out_ref[j, :cells, :] = block(OWNERS + device).astype(jnp.bfloat16)
        for half in range(2):
            rows = spare[half, pl.ds(device, OWNERS, stride=cells), :]
            out_ref[j, main:, 128 * half:128 * half + 128] = rows.astype(jnp.bfloat16)


def remap(items, tiles, weights, flux, devices, main):
    group = 16
    _, cells, tile = weights.shape
    channels = flux.shape[2]
    grid_spec = pltpu.PrefetchScalarGridSpec(
        num_scalar_prefetch=2,
        grid=(devices // group,),
        in_specs=[
            pl.BlockSpec(weights.shape, lambda i, *_: (0, 0, 0)),
            pl.BlockSpec(flux.shape, lambda i, *_: (0, 0, 0)),
        ],
        out_specs=pl.BlockSpec((group, main + OWNERS, channels), lambda i, *_: (i, 0, 0)),
        scratch_shapes=[pltpu.VMEM((2, OWNERS * cells, 128), jnp.float32)],
    )
    return pl.pallas_call(
        functools.partial(remap_body, group, main),
        grid_spec=grid_spec,
        out_shape=jax.ShapeDtypeStruct((devices, main + OWNERS, channels), jnp.bfloat16),
        compiler_params=pltpu.CompilerParams(vmem_limit_bytes=56 << 20),
        name="remap",
    )(items, tiles, far(weights), flux)


def spread(x_ref, flat):
    count, rows, _ = x_ref.shape

    def fill(s, carry):
        start = pl.multiple_of(s * rows, rows)
        value = x_ref[s].astype(jnp.float32)
        flat[0, pl.ds(start, rows), :] = value[:, :128]
        flat[1, pl.ds(start, rows), :] = value[:, 128:]
        return carry

    lax.fori_loop(0, count, fill, 0, unroll=8)


def part_body(turn_ref, rank_ref, bins_ref, x_ref, out_ref, flat, sums):
    sources, rows, _ = x_ref.shape
    spread(x_ref, flat)
    for h in range(rows):
        spot = jnp.broadcast_to(bins_ref[h:h + 1, :], (OB_DEV, sources))
        chosen = (spot == index((OB_DEV, sources), 0)).astype(jnp.bfloat16)
        for half in range(2):
            value = flat[half, pl.ds(h, sources, stride=rows), :].astype(jnp.bfloat16)
            sums[h, :, 128 * half:128 * half + 128] = jnp.dot(
                chosen, value, preferred_element_type=jnp.float32
            ).astype(jnp.bfloat16)

    def deal(d, carry):
        rank = rank_ref[d] - turn_ref[0] * OWNERS
        out_ref[d] = sums[jnp.clip(rank, 0, OWNERS - 1)]
        return carry

    lax.fori_loop(0, out_ref.shape[0], deal, 0, unroll=8)


def part_sum(turn, ranks, bins, arrived, main):
    devices, _, channels = arrived.shape
    grid_spec = pltpu.PrefetchScalarGridSpec(
        num_scalar_prefetch=2,
        grid=(1,),
        in_specs=[
            pl.BlockSpec((OWNERS, devices), lambda i, turn, _: (turn[0], 0)),
            pl.BlockSpec((devices, OWNERS, channels), lambda i, *_: (0, main // OWNERS, 0)),
        ],
        out_specs=pl.BlockSpec((devices, OB_DEV, channels), lambda i, *_: (0, 0, 0)),
        scratch_shapes=[
            pltpu.VMEM((2, devices * OWNERS, 128), jnp.float32),
            pltpu.VMEM((OWNERS, OB_DEV, channels), jnp.bfloat16),
        ],
    )
    return pl.pallas_call(
        part_body,
        grid_spec=grid_spec,
        out_shape=jax.ShapeDtypeStruct((devices, OB_DEV, channels), jnp.bfloat16),
        compiler_params=pltpu.CompilerParams(vmem_limit_bytes=14 << 20),
        name="part_sum",
    )(turn.reshape(1), ranks, bins, arrived)


def owner_body(group, bin_ref, x_ref, out_ref):
    step = pl.program_id(0)

    @pl.when(step == 0)
    def _():
        out_ref[...] = jnp.zeros_like(out_ref)

    for j in range(group):
        spot = bin_ref[step * group + j]

        @pl.when(spot >= 0)
        def _():
            out_ref[spot] += x_ref[j].astype(jnp.float32)


def owner_sum(bins, arrived, cells, group):
    devices, _, channels = arrived.shape
    grid_spec = pltpu.PrefetchScalarGridSpec(
        num_scalar_prefetch=1,
        grid=(devices // group,),
        in_specs=[pl.BlockSpec((group, cells, channels), lambda i, *_: (i, 0, 0))],
        out_specs=pl.BlockSpec((OB_DEV, cells, channels), lambda i, *_: (0, 0, 0)),
    )
    return pl.pallas_call(
        functools.partial(owner_body, group),
        grid_spec=grid_spec,
        out_shape=jax.ShapeDtypeStruct((OB_DEV, cells, channels), jnp.float32),
        compiler_params=pltpu.CompilerParams(vmem_limit_bytes=14 << 20),
        name="owner_sum",
    )(bins, arrived)


def late_body(rank_ref, total_ref, x_ref, out_ref, flat):
    rows = x_ref.shape[1]
    devices = x_ref.shape[0]
    out_ref[...] = total_ref[...]

    @pl.when((rank_ref[0] >= 0) & (rank_ref[0] < OWNERS))
    def _():
        spread(x_ref, flat)
        for b in range(rows):
            for half in range(2):
                lanes = slice(128 * half, 128 * half + 128)
                out_ref[b, :, lanes] += flat[half, pl.ds(b, devices, stride=rows), :]


def late_sum(rank, total, arrived):
    vmem = pl.BlockSpec(memory_space=pltpu.VMEM)
    return pl.pallas_call(
        late_body,
        in_specs=[pl.BlockSpec(memory_space=pltpu.SMEM), vmem, vmem],
        out_specs=vmem,
        out_shape=jax.ShapeDtypeStruct(total.shape, jnp.float32),
        scratch_shapes=[pltpu.VMEM((2, arrived.shape[0] * OB_DEV, 128), jnp.float32)],
        compiler_params=pltpu.CompilerParams(vmem_limit_bytes=14 << 20),
        name="late_sum",
    )(rank.reshape(1), total, arrived)


def exchange(value):
    return lax.all_to_all(value, BOTH, split_axis=0, concat_axis=0, tiled=True)


def shards(atmosphere, dw_kernel, norm_gain, w_in, w_out, w_flux, remap_weight, block_tile,
           block_owner, block_ocean):
    devices = lax.axis_size("lat") * lax.axis_size("lon")
    cells = remap_weight.shape[1]
    assert devices == cells == block_tile.shape[0]
    me = lax.axis_index(BOTH)
    own, code = route(block_owner, block_ocean, block_tile)
    table = exchange(code)
    mixer = (dw_kernel, norm_gain, w_in, w_out)
    rim1, rim2 = rims(atmosphere, *mixer)
    hidden = run_layer(atmosphere, rim1, 0, *mixer, None, 32)
    hidden, table = lax.optimization_barrier((hidden, table))
    rows, bins = plan(me, table, own)
    flux = run_layer(hidden, rim2, 1, *mixer, w_flux, 32)
    channels = flux.shape[1]
    flux = flux.reshape(-1, remap_weight.shape[2], channels)
    ranks = rows[16]
    my_rank = lax.dynamic_index_in_dim(ranks, me, keepdims=False)

    def spare_slots(turn):
        window = lambda row: lax.dynamic_slice_in_dim(row, turn * OWNERS, OWNERS)
        return window(rows[9]), window(rows[11])

    first = jnp.int32(0)
    spare_items, spare_tiles = rows[9, :OWNERS], rows[11, :OWNERS]
    sending = remap(
        jnp.concatenate([spare_items, own[0]]), jnp.concatenate([spare_tiles, own[2]]),
        remap_weight, flux, devices, cells,
    )
    arrived = exchange(sending)
    late = exchange(part_sum(first, ranks, bins, arrived, cells))
    total = owner_sum(rows[0], arrived, cells, 16)
    total = late_sum(my_rank, total, late)

    def more(state):
        return state[0] * OWNERS < rows[24, 0]

    def again(state):
        turn, total = state
        items, tiles = spare_slots(turn)
        arrived = exchange(remap(items, tiles, remap_weight, flux, devices, 0))
        late = exchange(part_sum(turn, ranks, bins, arrived, 0))
        return turn + 1, late_sum(my_rank - turn * OWNERS, total, late)

    _, total = lax.while_loop(more, again, (first + 1, total))
    return total.reshape(-1, channels)


def solution(mesh):
    placed = (
        P("lat", "lon", None),
        P(),
        P(),
        P(),
        P(),
        P(),
        P(BOTH, None, None),
        P(BOTH),
        P(BOTH, None),
        P(BOTH),
    )
    return jax.shard_map(
        shards, mesh=mesh, in_specs=placed, out_specs=P(BOTH, None), check_vma=False
    )
```

```python
import functools
import jax
import jax.numpy as jnp
from jax import lax
from jax.experimental import pallas as pl
from jax.experimental.pallas import tpu as pltpu
from jax.sharding import PartitionSpec as P

CAP = 2
OB_DEV = 16
OWNERS = 16


def far(value):
    return pltpu.with_memory_space_constraint(value, pltpu.HBM)

BOTH = ("lat", "lon")
PAD = 8
GELU_A = 0.7978845608028654
GELU_B = 0.044715 * GELU_A


def shift(value, axis, periodic):
    count = lax.axis_size(axis)
    forward = [(i, i + 1) for i in range(count - 1)]
    if periodic:
        forward.append((count - 1, 0))
    backward = [(target, source) for source, target in forward]
    return (
        lax.ppermute(value[1], axis, forward),
        lax.ppermute(value[0], axis, backward),
    )


def mix(depth, gain_ref, win_ref, wout_ref):
    flat = depth.astype(jnp.bfloat16).astype(jnp.float32)
    mean_sq = jnp.mean(flat * flat, axis=-1, keepdims=True)
    normed = (flat * lax.rsqrt(mean_sq + 1e-06) * gain_ref[...]).astype(jnp.bfloat16)
    wide = jnp.dot(normed, win_ref[...], preferred_element_type=jnp.float32)
    inner = wide * (GELU_A + GELU_B * (wide * wide))
    hidden = (wide * (0.5 + 0.5 * jnp.tanh(inner))).astype(jnp.bfloat16)
    return flat + jnp.dot(hidden, wout_ref[...], preferred_element_type=jnp.float32)


def layer_body(rows, cols, steps, with_flux, *refs):
    if with_flux:
        (x_ref, prev_ref, next_ref, top_ref, bot_ref, left_ref, right_ref, kern_ref, gain_ref,
         win_ref, wout_ref, wflux_ref, out_ref, xs, dep) = refs
    else:
        (x_ref, prev_ref, next_ref, top_ref, bot_ref, left_ref, right_ref, kern_ref, gain_ref,
         win_ref, wout_ref, out_ref, edge_ref, xs, dep) = refs
    step = pl.program_id(0)
    half = cols // 2

    def put(slot, value):
        value = value.astype(jnp.float32)
        xs[slot, 0, PAD:PAD + cols, :] = value[:, :128]
        xs[slot, 1, PAD:PAD + cols, :] = value[:, 128:]

    first = jnp.where(step == 0, top_ref[...].astype(jnp.float32), prev_ref[0].astype(jnp.float32))
    last = jnp.where(
        step == steps - 1, bot_ref[...].astype(jnp.float32), next_ref[0].astype(jnp.float32)
    )
    put(0, first)
    put(2 * rows + 1, last)
    for r in range(2 * rows):
        put(r + 1, x_ref[r])
    base = pl.multiple_of(step * (2 * rows), 2 * rows)
    near = left_ref[pl.ds(base, 2 * rows + 8), :]
    after = right_ref[pl.ds(base, 2 * rows + 8), :]
    for r in range(2 * rows + 2):
        for h in range(2):
            lanes = slice(128 * h, 128 * h + 128)
            xs[r, h, PAD - 1:PAD, :] = near[r:r + 1, lanes]
            xs[r, h, PAD + cols:PAD + cols + 1, :] = after[r:r + 1, lanes]
    for h in range(2):
        lanes = slice(128 * h, 128 * h + 128)
        for k in range(rows):
            total = jnp.zeros((half, 128), jnp.float32)
            for p in range(4):
                for q in range(4):
                    window = xs[2 * k + p, h, pl.ds(PAD - 1 + q, half, stride=2), :]
                    total = total + window * kern_ref[4 * p + q:4 * p + q + 1, lanes]
            dep[k * half:(k + 1) * half, lanes] = total
    mixed = mix(dep[...], gain_ref, win_ref, wout_ref)
    if with_flux:
        out_ref[...] = jnp.dot(
            mixed.astype(jnp.bfloat16), wflux_ref[...], preferred_element_type=jnp.float32
        ).astype(jnp.bfloat16)
    else:
        out_ref[...] = mixed.astype(jnp.bfloat16).reshape(rows, half, mixed.shape[1])


def rim_body(edge_ref, from_left, from_right, left_ref, right_ref, top_ref, bot_ref, first_ref,
             last_ref, kern_ref, gain_ref, win_ref, wout_ref, left1, right1, left2, right2, top2,
             bot2, tall, wide, cells):
    rows = left_ref.shape[1] - 16
    cols = first_ref.shape[1]
    half_cols = cols // 2
    side = left2.shape[0]
    halves = [(h, slice(128 * h, 128 * h + 128)) for h in range(2)]
    strips = [(from_left, c) for c in range(3)] + [(left_ref, 0)]
    strips += [(right_ref, 2)] + [(from_right, c) for c in range(3)]
    for n, (ref, c) in enumerate(strips):
        value = ref[c].astype(jnp.float32)
        for h, lanes in halves:
            tall[n, h, PAD:PAD + rows, :] = value[:rows, lanes]
            tall[n, h, PAD - 3:PAD, :] = value[rows:rows + 3, lanes]
            tall[n, h, PAD + rows:PAD + rows + 3, :] = value[rows + 3:rows + 6, lanes]
            tall[n, h, PAD + rows + 3:, :] = jnp.zeros(
                (tall.shape[2] - PAD - rows - 3, 128), jnp.float32
            )
    for h, lanes in halves:
        left1[:, lanes] = tall[2, h, PAD - 1:PAD - 1 + left1.shape[0], :]
        right1[:, lanes] = tall[5, h, PAD - 1:PAD - 1 + right1.shape[0], :]
    lines = [(top_ref[i], i - 3) for i in range(3)] + [(first_ref[0], 0)]
    lines += [(last_ref[0], rows - 1)] + [(bot_ref[i], rows + i) for i in range(3)]
    for n, (value, row) in enumerate(lines):
        value = value.astype(jnp.float32)
        at = PAD + row
        for h, lanes in halves:
            wide[n, h, PAD:PAD + cols, :] = value[:, lanes]
            wide[n, h, PAD - 1:PAD, :] = tall[2, h, at:at + 1, :]
            wide[n, h, PAD + cols:PAD + cols + 1, :] = tall[5, h, at:at + 1, :]
    for h, lanes in halves:
        for part in range(2):
            total = jnp.zeros((side, 128), jnp.float32)
            line = jnp.zeros((half_cols, 128), jnp.float32)
            for p in range(4):
                for q in range(4):
                    tap = kern_ref[4 * p + q:4 * p + q + 1, lanes]
                    total = total + tall[4 * part + q, h, pl.ds(PAD - 3 + p, side, stride=2), :] * tap
                    line = line + wide[4 * part + p, h, pl.ds(PAD - 1 + q, half_cols, stride=2), :] * tap
            cells[side * part:side * part + side, lanes] = total
            at = 2 * side + half_cols * part
            cells[at:at + half_cols, lanes] = line
    mixed = mix(cells[...], gain_ref, win_ref, wout_ref).astype(jnp.bfloat16).astype(jnp.float32)
    place = index((side, mixed.shape[1]), 0)
    outside = ((place == 0) & (edge_ref[0] > 0)) | ((place == rows // 2 + 1) & (edge_ref[1] > 0))
    left2[...] = jnp.where(outside, 0.0, mixed[:side])
    right2[...] = jnp.where(outside, 0.0, mixed[side:2 * side])
    at = 2 * side
    top2[...] = jnp.where(edge_ref[0] > 0, 0.0, mixed[at:at + half_cols]).astype(jnp.bfloat16)
    bot2[...] = jnp.where(edge_ref[1] > 0, 0.0, mixed[at + half_cols:]).astype(jnp.bfloat16)


def rims(current, dw_kernel, norm_gain, w_in, w_out):
    rows, cols, channels = current.shape
    hid = w_in.shape[2]
    top, bot = shift((current[:3], current[-3:]), "lat", False)
    fill = jnp.zeros((3, 10, channels), current.dtype)
    sides = [
        jnp.concatenate(
            [jnp.swapaxes(part[:, c:c + 3], 0, 1) for part in (current, top, bot)] + [fill], axis=1
        )
        for c in (0, cols - 3)
    ]
    from_left, from_right = shift(sides, "lon", True)
    lat = lax.axis_index("lat")
    edge = jnp.stack([lat == 0, lat == lax.axis_size("lat") - 1]).astype(jnp.int32)
    whole = lambda shape: pl.BlockSpec(shape, lambda i: (0,) * len(shape))
    pick = lambda shape: pl.BlockSpec((None,) + shape, lambda i: (0,) * (len(shape) + 1))
    side = rows // 2 + 8
    outs = [(rows + 8, jnp.float32)] * 2 + [(side, jnp.float32)] * 2 + [(cols // 2, jnp.bfloat16)] * 2
    left1, right1, left2, right2, top2, bot2 = pl.pallas_call(
        rim_body,
        grid=(1,),
        in_specs=[pl.BlockSpec(memory_space=pltpu.SMEM)]
        + [whole(sides[0].shape)] * 4
        + [whole(top.shape)] * 2
        + [
            pl.BlockSpec((1, cols, channels), lambda i: (0, 0, 0)),
            pl.BlockSpec((1, cols, channels), lambda i: (rows - 1, 0, 0)),
            pick((16, channels)),
            pick((1, channels)),
            pick((channels, hid)),
            pick((hid, channels)),
        ],
        out_specs=[whole((count, channels)) for count, _ in outs],
        out_shape=[jax.ShapeDtypeStruct((count, channels), kind) for count, kind in outs],
        scratch_shapes=[
            pltpu.VMEM((8, 2, rows + 4 * PAD, 128), jnp.float32),
            pltpu.VMEM((8, 2, cols + 2 * PAD, 128), jnp.float32),
            pltpu.VMEM((2 * side + cols, channels), jnp.float32),
        ],
        compiler_params=pltpu.CompilerParams(vmem_limit_bytes=20 << 20),
        name="rim",
    )(edge, from_left, from_right, *sides, top, bot, far(current), far(current), dw_kernel,
      norm_gain[:, None, :], far(w_in), far(w_out))
    return (top[-1], bot[0], left1, right1), (top2, bot2, left2, right2)


def run_layer(current, halo, layer, dw_kernel, norm_gain, w_in, w_out, w_flux, rows):
    in_rows, in_cols, channels = current.shape
    out_rows, out_cols = in_rows // 2, in_cols // 2
    hid = w_in.shape[2]
    steps = out_rows // rows
    with_flux = w_flux is not None
    whole = lambda shape: pl.BlockSpec(shape, lambda i: (0,) * len(shape))
    pick = lambda shape: pl.BlockSpec((None,) + shape, lambda i: (layer,) + (0,) * len(shape))
    in_specs = [
        pl.BlockSpec((2 * rows, in_cols, channels), lambda i: (i, 0, 0)),
        pl.BlockSpec((1, in_cols, channels), lambda i: (jnp.maximum(2 * rows * i - 1, 0), 0, 0)),
        pl.BlockSpec(
            (1, in_cols, channels), lambda i: (jnp.minimum(2 * rows * (i + 1), in_rows - 1), 0, 0)
        ),
        whole((in_cols, channels)),
        whole((in_cols, channels)),
        whole((in_rows + 8, channels)),
        whole((in_rows + 8, channels)),
        pick((16, channels)),
        pick((1, channels)),
        pick((channels, hid)),
        pick((hid, channels)),
    ]
    field = current if with_flux else far(current)
    operands = [field, field, field, *halo, dw_kernel, norm_gain[:, None, :], far(w_in), far(w_out)]
    cells = out_rows * out_cols
    if with_flux:
        in_specs.append(whole((channels, channels)))
        operands.append(w_flux)
        out_specs = pl.BlockSpec((rows * out_cols, channels), lambda i: (i, 0))
        out_shape = jax.ShapeDtypeStruct((cells, channels), jnp.bfloat16)
    else:
        out_specs = pl.BlockSpec((rows, out_cols, channels), lambda i: (i, 0, 0))
        out_shape = jax.ShapeDtypeStruct((out_rows, out_cols, channels), jnp.bfloat16)

    def body(*refs):
        if with_flux:
            layer_body(rows, in_cols, steps, True, *refs)
        else:
            layer_body(rows, in_cols, steps, False, *refs[:12], None, *refs[12:])

    return pl.pallas_call(
        body,
        grid=(steps,),
        in_specs=in_specs,
        out_specs=out_specs,
        out_shape=out_shape,
        scratch_shapes=[
            pltpu.VMEM((2 * rows + 2, 2, in_cols + 2 * PAD, 128), jnp.float32),
            pltpu.VMEM((rows * out_cols, channels), jnp.float32),
        ],
        compiler_params=pltpu.CompilerParams(vmem_limit_bytes=28 << 20),
        cost_estimate=pl.CostEstimate(
            flops=cells * channels * hid // 4, transcendentals=0,
            bytes_accessed=2 * (in_rows * in_cols + cells) * channels,
        ),
        name="layer",
    )(*operands)


def index(shape, dim):
    return lax.broadcasted_iota(jnp.int32, shape, dim)


def matmul(lhs, rhs, rhs_dim):
    return lax.dot_general(
        lhs.astype(jnp.float32), rhs.astype(jnp.float32), (((1,), (rhs_dim,)), ((), ())),
        preferred_element_type=jnp.float32,
    )


def column_of(row):
    size = row.shape[1]
    square = (size, size)
    diagonal = index(square, 0) == index(square, 1)
    return jnp.sum(jnp.where(diagonal, jnp.broadcast_to(row, square), 0), axis=1, keepdims=True)


def route_body(owner_ref, ocean_ref, tile_ref, out_ref, code_ref):
    owner_row = owner_ref[...]
    blocks = owner_row.shape[1]
    owner, ocean, tile = (column_of(ref[...]) for ref in (owner_ref, ocean_ref, tile_ref))
    square = (blocks, blocks)
    same = (owner == owner_row) & (index(square, 1) < index(square, 0))
    rank = jnp.sum(same.astype(jnp.int32), axis=1, keepdims=True)
    mine = owner == index(square, 1)
    code = jnp.zeros((1, blocks), jnp.int32)
    for r in range(CAP):
        hit = (mine & (rank == r)).astype(jnp.int32)
        sums = lambda column: jnp.sum(hit * column, axis=0, keepdims=True)
        code = code * 32 + sums(ocean + 1)
        out_ref[r:r + 1, :] = sums(index((blocks, 1), 0))
        out_ref[2 + r:3 + r, :] = sums(tile)
    out_ref[4:8, :] = jnp.zeros((4, blocks), jnp.int32)
    code_ref[...] = jnp.broadcast_to(code, code_ref.shape)


def route(owner, ocean, tile):
    blocks = owner.shape[0]
    return pl.pallas_call(
        route_body,
        out_shape=[
            jax.ShapeDtypeStruct((8, blocks), jnp.int32),
            jax.ShapeDtypeStruct((blocks, blocks), jnp.int32),
        ],
        name="route",
    )(owner.reshape(1, blocks), ocean.reshape(1, blocks), tile.reshape(1, blocks))


def plan_body(me_ref, table_ref, own_ref, row_ref, bins_ref):
    code = table_ref[...]
    devices = code.shape[0]
    square = (devices, devices)
    spare = code & 31
    hot = jnp.max(spare, axis=0, keepdims=True) > 0
    hot8 = jnp.broadcast_to(hot, (8, devices)).astype(jnp.float32)
    before = (index(square, 0) < index(square, 1)).astype(jnp.float32)
    rank = matmul(hot8, before, 0).astype(jnp.int32)
    listed = (jnp.broadcast_to(hot, square) & (rank[:1] == index(square, 0))).astype(jnp.float32)
    bins_ref[...] = matmul(listed, spare, 1).astype(jnp.int32) - 1
    me = (index((8, devices), 1) == me_ref[0]).astype(jnp.float32)
    row_ref[0:8] = matmul(me, code >> 5, 1).astype(jnp.int32) - 1
    row_ref[8:16] = matmul(own_ref[...], listed, 1).astype(jnp.int32)
    row_ref[16:24] = jnp.where(hot8 > 0, rank, -1)
    row_ref[24:32] = jnp.broadcast_to(
        jnp.sum(hot8, axis=1, keepdims=True).astype(jnp.int32), (8, devices)
    )


def plan(me, table, own):
    devices = table.shape[0]
    vmem = pl.BlockSpec(memory_space=pltpu.VMEM)
    return pl.pallas_call(
        plan_body,
        in_specs=[pl.BlockSpec(memory_space=pltpu.SMEM), vmem, vmem],
        out_specs=[vmem, vmem],
        out_shape=[
            jax.ShapeDtypeStruct((32, devices), jnp.int32),
            jax.ShapeDtypeStruct((devices, devices), jnp.int32),
        ],
        name="plan",
    )(me.reshape(1), table, own)


def spare_body(turn_ref, row_ref, w_ref, flux_ref, out_ref, weights, spare, sems):
    cells = w_ref.shape[1]
    first = turn_ref[0] * OWNERS
    copies = [
        pltpu.make_async_copy(w_ref.at[row_ref[9, first + h]], weights.at[h], sems.at[h])
        for h in range(OWNERS)
    ]
    for copy in copies:
        copy.start()
    for h, copy in enumerate(copies):
        copy.wait()
        rows = slice(h * cells, h * cells + cells)
        value = jnp.dot(
            weights[h], flux_ref[row_ref[11, first + h]], preferred_element_type=jnp.float32
        )
        spare[0, rows, :] = value[:, :128]
        spare[1, rows, :] = value[:, 128:]
    for device in range(out_ref.shape[0]):
        for half in range(2):
            rows = spare[half, pl.ds(device, OWNERS, stride=cells), :]
            out_ref[device, :, 128 * half:128 * half + 128] = rows.astype(jnp.bfloat16)


def remap_spare(turn, rows, weights, flux):
    _, cells, tile = weights.shape
    channels = flux.shape[2]
    out = (cells, OWNERS, channels)
    grid_spec = pltpu.PrefetchScalarGridSpec(
        num_scalar_prefetch=2,
        grid=(1,),
        in_specs=[
            pl.BlockSpec(memory_space=pl.ANY),
            pl.BlockSpec(flux.shape, lambda i, *_: (0, 0, 0)),
        ],
        out_specs=pl.BlockSpec(out, lambda i, *_: (0, 0, 0)),
        scratch_shapes=[
            pltpu.VMEM((OWNERS, cells, tile), jnp.bfloat16),
            pltpu.VMEM((2, OWNERS * cells, 128), jnp.float32),
            pltpu.SemaphoreType.DMA((OWNERS,)),
        ],
    )
    return pl.pallas_call(
        spare_body,
        grid_spec=grid_spec,
        out_shape=jax.ShapeDtypeStruct(out, jnp.bfloat16),
        compiler_params=pltpu.CompilerParams(vmem_limit_bytes=16 << 20),
        name="remap_spare",
    )(turn.reshape(1), rows, far(weights), flux)


def remap_body(group, own_ref, w_ref, flux_ref, out_ref):
    base = pl.program_id(0) * group
    for j in range(group):
        out_ref[j] = jnp.dot(
            w_ref[own_ref[0, base + j]], flux_ref[own_ref[2, base + j]],
            preferred_element_type=jnp.float32,
        ).astype(jnp.bfloat16)


def remap(own, weights, flux):
    group = 16
    devices, cells, tile = weights.shape
    channels = flux.shape[2]
    grid_spec = pltpu.PrefetchScalarGridSpec(
        num_scalar_prefetch=1,
        grid=(devices // group,),
        in_specs=[
            pl.BlockSpec(weights.shape, lambda i, *_: (0, 0, 0)),
            pl.BlockSpec(flux.shape, lambda i, *_: (0, 0, 0)),
        ],
        out_specs=pl.BlockSpec((group, cells, channels), lambda i, *_: (i, 0, 0)),
    )
    return pl.pallas_call(
        functools.partial(remap_body, group),
        grid_spec=grid_spec,
        out_shape=pltpu.HBM((devices, cells + OB_DEV, channels), jnp.bfloat16),
        compiler_params=pltpu.CompilerParams(vmem_limit_bytes=56 << 20),
        name="remap",
    )(own, far(weights), flux)


def spread(x_ref, flat):
    count, rows, _ = x_ref.shape

    def fill(s, carry):
        start = pl.multiple_of(s * rows, rows)
        value = x_ref[s].astype(jnp.float32)
        flat[0, pl.ds(start, rows), :] = value[:, :128]
        flat[1, pl.ds(start, rows), :] = value[:, 128:]
        return carry

    lax.fori_loop(0, count, fill, 0, unroll=8)


def part_body(turn_ref, row_ref, bins_ref, x_ref, *refs):
    out_ref, flat, sums = refs[-3:]
    sources, rows, _ = x_ref.shape
    spread(x_ref, flat)
    for h in range(rows):
        spot = jnp.broadcast_to(bins_ref[h:h + 1, :], (OB_DEV, sources))
        chosen = (spot == index((OB_DEV, sources), 0)).astype(jnp.bfloat16)
        for half in range(2):
            value = flat[half, pl.ds(h, sources, stride=rows), :].astype(jnp.bfloat16)
            sums[h, :, 128 * half:128 * half + 128] = jnp.dot(
                chosen, value, preferred_element_type=jnp.float32
            ).astype(jnp.bfloat16)

    def deal(d, carry):
        rank = row_ref[16, d] - turn_ref[0] * OWNERS
        out_ref[d] = sums[jnp.clip(rank, 0, OWNERS - 1)]
        return carry

    lax.fori_loop(0, out_ref.shape[0], deal, 0, unroll=8)


def part_sum(turn, rows, bins, arrived, slots):
    devices, _, channels = arrived.shape
    in_specs = [
        pl.BlockSpec((OWNERS, devices), lambda i, turn, _: (turn[0], 0)),
        pl.BlockSpec((devices, OWNERS, channels), lambda i, *_: (0, 0, 0)),
    ]
    operands = [turn.reshape(1), rows, bins, arrived]
    tail, aliases = 0, {}
    out_shape = jax.ShapeDtypeStruct((devices, OB_DEV, channels), jnp.bfloat16)
    if slots is not None:
        in_specs.append(pl.BlockSpec(memory_space=pl.ANY))
        operands.append(slots)
        tail, aliases = slots.shape[1] // OB_DEV - 1, {4: 0}
        out_shape = pltpu.HBM(slots.shape, jnp.bfloat16)
    grid_spec = pltpu.PrefetchScalarGridSpec(
        num_scalar_prefetch=2,
        grid=(1,),
        in_specs=in_specs,
        out_specs=pl.BlockSpec((devices, OB_DEV, channels), lambda i, *_: (0, tail, 0)),
        scratch_shapes=[
            pltpu.VMEM((2, devices * OWNERS, 128), jnp.float32),
            pltpu.VMEM((OWNERS, OB_DEV, channels), jnp.bfloat16),
        ],
    )
    return pl.pallas_call(
        part_body,
        grid_spec=grid_spec,
        out_shape=out_shape,
        input_output_aliases=aliases,
        compiler_params=pltpu.CompilerParams(vmem_limit_bytes=14 << 20),
        name="part_sum",
    )(*operands)


def owner_body(group, me_ref, row_ref, x_ref, out_ref, total, flat):
    step = pl.program_id(0)
    rows = OB_DEV
    cells = out_ref.shape[1]
    devices = pl.num_programs(0) * group
    rank = row_ref[16, me_ref[0]]
    served = (rank >= 0) & (rank < OWNERS)

    @pl.when(step == 0)
    def _():
        total[...] = jnp.zeros_like(total)

    for j in range(group):
        source = step * group + j
        spot = row_ref[0, source]
        spot = jnp.where(spot < 0, OB_DEV, spot)
        total[spot] += x_ref[j, :cells, :].astype(jnp.float32)
        start = pl.multiple_of(source * rows, rows)
        value = x_ref[j, cells:, :].astype(jnp.float32)
        flat[0, pl.ds(start, rows), :] = value[:, :128]
        flat[1, pl.ds(start, rows), :] = value[:, 128:]

    last = step == pl.num_programs(0) - 1

    @pl.when(last & jnp.logical_not(served))
    def _():
        out_ref[...] = total[:OB_DEV]

    @pl.when(last & served)
    def _():
        for b in range(OB_DEV):
            for half in range(2):
                lanes = slice(128 * half, 128 * half + 128)
                late = flat[half, pl.ds(b, cells, stride=rows), :]
                out_ref[b, :, lanes] = total[b, :, lanes] + late


def owner_sum(me, rows, arrived, group):
    devices, both, channels = arrived.shape
    cells = both - OB_DEV
    grid_spec = pltpu.PrefetchScalarGridSpec(
        num_scalar_prefetch=2,
        grid=(devices // group,),
        in_specs=[pl.BlockSpec((group, both, channels), lambda i, *_: (i, 0, 0))],
        out_specs=pl.BlockSpec((OB_DEV, cells, channels), lambda i, *_: (0, 0, 0)),
        scratch_shapes=[
            pltpu.VMEM((OB_DEV + 1, cells, channels), jnp.float32),
            pltpu.VMEM((2, devices * OB_DEV, 128), jnp.float32),
        ],
    )
    return pl.pallas_call(
        functools.partial(owner_body, group),
        grid_spec=grid_spec,
        out_shape=jax.ShapeDtypeStruct((OB_DEV, cells, channels), jnp.float32),
        compiler_params=pltpu.CompilerParams(vmem_limit_bytes=24 << 20),
        name="owner_sum",
    )(me.reshape(1), rows, arrived)


def late_body(rank_ref, total_ref, x_ref, out_ref, flat):
    rows = x_ref.shape[1]
    devices = x_ref.shape[0]
    out_ref[...] = total_ref[...]

    @pl.when((rank_ref[0] >= 0) & (rank_ref[0] < OWNERS))
    def _():
        spread(x_ref, flat)
        for b in range(rows):
            for half in range(2):
                lanes = slice(128 * half, 128 * half + 128)
                out_ref[b, :, lanes] += flat[half, pl.ds(b, devices, stride=rows), :]


def late_sum(rank, total, arrived):
    vmem = pl.BlockSpec(memory_space=pltpu.VMEM)
    return pl.pallas_call(
        late_body,
        in_specs=[pl.BlockSpec(memory_space=pltpu.SMEM), vmem, vmem],
        out_specs=vmem,
        out_shape=jax.ShapeDtypeStruct(total.shape, jnp.float32),
        scratch_shapes=[pltpu.VMEM((2, arrived.shape[0] * OB_DEV, 128), jnp.float32)],
        compiler_params=pltpu.CompilerParams(vmem_limit_bytes=14 << 20),
        name="late_sum",
    )(rank.reshape(1), total, arrived)


def exchange(value):
    return lax.all_to_all(value, BOTH, split_axis=0, concat_axis=0, tiled=True)


def shards(atmosphere, dw_kernel, norm_gain, w_in, w_out, w_flux, remap_weight, block_tile,
           block_owner, block_ocean):
    devices = lax.axis_size("lat") * lax.axis_size("lon")
    cells = remap_weight.shape[1]
    assert devices == cells == block_tile.shape[0]
    me = lax.axis_index(BOTH)
    own, code = route(block_owner, block_ocean, block_tile)
    table = exchange(code)
    mixer = (dw_kernel, norm_gain, w_in, w_out)
    rim1, rim2 = rims(atmosphere, *mixer)
    hidden = run_layer(atmosphere, rim1, 0, *mixer, None, 32)
    hidden, table = lax.optimization_barrier((hidden, table))
    rows, bins = plan(me, table, own)
    flux = run_layer(hidden, rim2, 1, *mixer, w_flux, 32)
    channels = flux.shape[1]
    flux = flux.reshape(-1, remap_weight.shape[2], channels)
    first = jnp.int32(0)
    count = rows[24, 0]
    parts = exchange(remap_spare(first, rows, remap_weight, flux))
    sending = part_sum(first, rows, bins, parts, remap(own, remap_weight, flux))
    total = owner_sum(me, rows, exchange(sending), 16)

    def more(state):
        return state[0] * OWNERS < count

    def again(state):
        turn, total = state
        parts = exchange(remap_spare(turn, rows, remap_weight, flux))
        late = exchange(part_sum(turn, rows, bins, parts, None))
        rank = lax.dynamic_index_in_dim(rows[16], me, keepdims=False)
        return turn + 1, late_sum(rank - turn * OWNERS, total, late)

    _, total = lax.while_loop(more, again, (first + 1, total))
    return total.reshape(-1, channels)


def solution(mesh):
    placed = (
        P("lat", "lon", None),
        P(),
        P(),
        P(),
        P(),
        P(),
        P(BOTH, None, None),
        P(BOTH),
        P(BOTH, None),
        P(BOTH),
    )
    return jax.shard_map(
        shards, mesh=mesh, in_specs=placed, out_specs=P(BOTH, None), check_vma=False
    )
```

```python
import functools
import jax
import jax.numpy as jnp
from jax import lax
from jax.experimental import pallas as pl
from jax.experimental.pallas import tpu as pltpu
from jax.sharding import PartitionSpec as P

CAP = 2
OB_DEV = 16
OWNERS = 16


def far(value):
    return pltpu.with_memory_space_constraint(value, pltpu.HBM)

BOTH = ("lat", "lon")
PAD = 8
GELU_A = 0.7978845608028654
GELU_B = 0.044715 * GELU_A


def shift(value, axis, periodic):
    count = lax.axis_size(axis)
    forward = [(i, i + 1) for i in range(count - 1)]
    if periodic:
        forward.append((count - 1, 0))
    backward = [(target, source) for source, target in forward]
    return (
        lax.ppermute(value[1], axis, forward),
        lax.ppermute(value[0], axis, backward),
    )


def mix(depth, gain_ref, win_ref, wout_ref):
    flat = depth.astype(jnp.bfloat16).astype(jnp.float32)
    mean_sq = jnp.mean(flat * flat, axis=-1, keepdims=True)
    normed = (flat * lax.rsqrt(mean_sq + 1e-06) * gain_ref[...]).astype(jnp.bfloat16)
    wide = jnp.dot(normed, win_ref[...], preferred_element_type=jnp.float32)
    inner = wide * (GELU_A + GELU_B * (wide * wide))
    hidden = (wide * (0.5 + 0.5 * jnp.tanh(inner))).astype(jnp.bfloat16)
    return flat + jnp.dot(hidden, wout_ref[...], preferred_element_type=jnp.float32)


def layer_body(rows, cols, steps, with_flux, *refs):
    if with_flux:
        (x_ref, prev_ref, next_ref, top_ref, bot_ref, left_ref, right_ref, kern_ref, gain_ref,
         win_ref, wout_ref, wflux_ref, row_ref, remap_ref, out_ref, spare_ref, xs, dep, flux, weights,
         spare, sems) = refs
    else:
        (x_ref, prev_ref, next_ref, top_ref, bot_ref, left_ref, right_ref, kern_ref, gain_ref,
         win_ref, wout_ref, out_ref, edge_ref, xs, dep) = refs
    step = pl.program_id(0)
    half = cols // 2
    if with_flux:
        copies = spare_copies(0, row_ref, remap_ref, weights, sems)

        @pl.when(step == 0)
        def _():
            for copy in copies:
                copy.start()

    def put(slot, value):
        value = value.astype(jnp.float32)
        xs[slot, 0, PAD:PAD + cols, :] = value[:, :128]
        xs[slot, 1, PAD:PAD + cols, :] = value[:, 128:]

    first = jnp.where(step == 0, top_ref[...].astype(jnp.float32), prev_ref[0].astype(jnp.float32))
    last = jnp.where(
        step == steps - 1, bot_ref[...].astype(jnp.float32), next_ref[0].astype(jnp.float32)
    )
    put(0, first)
    put(2 * rows + 1, last)
    for r in range(2 * rows):
        put(r + 1, x_ref[r])
    base = pl.multiple_of(step * (2 * rows), 2 * rows)
    near = left_ref[pl.ds(base, 2 * rows + 8), :]
    after = right_ref[pl.ds(base, 2 * rows + 8), :]
    for r in range(2 * rows + 2):
        for h in range(2):
            lanes = slice(128 * h, 128 * h + 128)
            xs[r, h, PAD - 1:PAD, :] = near[r:r + 1, lanes]
            xs[r, h, PAD + cols:PAD + cols + 1, :] = after[r:r + 1, lanes]
    for h in range(2):
        lanes = slice(128 * h, 128 * h + 128)
        for k in range(rows):
            total = jnp.zeros((half, 128), jnp.float32)
            for p in range(4):
                for q in range(4):
                    window = xs[2 * k + p, h, pl.ds(PAD - 1 + q, half, stride=2), :]
                    total = total + window * kern_ref[4 * p + q:4 * p + q + 1, lanes]
            dep[k * half:(k + 1) * half, lanes] = total
    mixed = mix(dep[...], gain_ref, win_ref, wout_ref)
    if with_flux:
        value = jnp.dot(
            mixed.astype(jnp.bfloat16), wflux_ref[...], preferred_element_type=jnp.float32
        ).astype(jnp.bfloat16)
        out_ref[...] = value
        count = rows * half
        flux[pl.ds(pl.multiple_of(step * count, count), count), :] = value
        cells = weights.shape[2]

        @pl.when(step == steps - 1)
        def _():
            for copy in copies:
                copy.wait()
            tile_of = lambda tile: flux[pl.ds(pl.multiple_of(tile * cells, cells), cells), :]
            spare_rows(0, row_ref, weights, tile_of, spare_ref, spare)

    else:
        out_ref[...] = mixed.astype(jnp.bfloat16).reshape(rows, half, mixed.shape[1])


def rim_body(edge_ref, from_left, from_right, left_ref, right_ref, top_ref, bot_ref, first_ref,
             last_ref, kern_ref, gain_ref, win_ref, wout_ref, left1, right1, left2, right2, top2,
             bot2, tall, wide, cells):
    rows = left_ref.shape[1] - 16
    cols = first_ref.shape[1]
    half_cols = cols // 2
    side = left2.shape[0]
    halves = [(h, slice(128 * h, 128 * h + 128)) for h in range(2)]
    strips = [(from_left, c) for c in range(3)] + [(left_ref, 0)]
    strips += [(right_ref, 2)] + [(from_right, c) for c in range(3)]
    for n, (ref, c) in enumerate(strips):
        value = ref[c].astype(jnp.float32)
        for h, lanes in halves:
            tall[n, h, PAD:PAD + rows, :] = value[:rows, lanes]
            tall[n, h, PAD - 3:PAD, :] = value[rows:rows + 3, lanes]
            tall[n, h, PAD + rows:PAD + rows + 3, :] = value[rows + 3:rows + 6, lanes]
            tall[n, h, PAD + rows + 3:, :] = jnp.zeros(
                (tall.shape[2] - PAD - rows - 3, 128), jnp.float32
            )
    for h, lanes in halves:
        left1[:, lanes] = tall[2, h, PAD - 1:PAD - 1 + left1.shape[0], :]
        right1[:, lanes] = tall[5, h, PAD - 1:PAD - 1 + right1.shape[0], :]
    lines = [(top_ref[i], i - 3) for i in range(3)] + [(first_ref[0], 0)]
    lines += [(last_ref[0], rows - 1)] + [(bot_ref[i], rows + i) for i in range(3)]
    for n, (value, row) in enumerate(lines):
        value = value.astype(jnp.float32)
        at = PAD + row
        for h, lanes in halves:
            wide[n, h, PAD:PAD + cols, :] = value[:, lanes]
            wide[n, h, PAD - 1:PAD, :] = tall[2, h, at:at + 1, :]
            wide[n, h, PAD + cols:PAD + cols + 1, :] = tall[5, h, at:at + 1, :]
    for h, lanes in halves:
        for part in range(2):
            total = jnp.zeros((side, 128), jnp.float32)
            line = jnp.zeros((half_cols, 128), jnp.float32)
            for p in range(4):
                for q in range(4):
                    tap = kern_ref[4 * p + q:4 * p + q + 1, lanes]
                    total = total + tall[4 * part + q, h, pl.ds(PAD - 3 + p, side, stride=2), :] * tap
                    line = line + wide[4 * part + p, h, pl.ds(PAD - 1 + q, half_cols, stride=2), :] * tap
            cells[side * part:side * part + side, lanes] = total
            at = 2 * side + half_cols * part
            cells[at:at + half_cols, lanes] = line
    mixed = mix(cells[...], gain_ref, win_ref, wout_ref).astype(jnp.bfloat16).astype(jnp.float32)
    place = index((side, mixed.shape[1]), 0)
    outside = ((place == 0) & (edge_ref[0] > 0)) | ((place == rows // 2 + 1) & (edge_ref[1] > 0))
    left2[...] = jnp.where(outside, 0.0, mixed[:side])
    right2[...] = jnp.where(outside, 0.0, mixed[side:2 * side])
    at = 2 * side
    top2[...] = jnp.where(edge_ref[0] > 0, 0.0, mixed[at:at + half_cols]).astype(jnp.bfloat16)
    bot2[...] = jnp.where(edge_ref[1] > 0, 0.0, mixed[at + half_cols:]).astype(jnp.bfloat16)


def rims(current, dw_kernel, norm_gain, w_in, w_out):
    rows, cols, channels = current.shape
    hid = w_in.shape[2]
    top, bot = shift((current[:3], current[-3:]), "lat", False)
    fill = jnp.zeros((3, 10, channels), current.dtype)
    sides = [
        jnp.concatenate(
            [jnp.swapaxes(part[:, c:c + 3], 0, 1) for part in (current, top, bot)] + [fill], axis=1
        )
        for c in (0, cols - 3)
    ]
    from_left, from_right = shift(sides, "lon", True)
    lat = lax.axis_index("lat")
    edge = jnp.stack([lat == 0, lat == lax.axis_size("lat") - 1]).astype(jnp.int32)
    whole = lambda shape: pl.BlockSpec(shape, lambda i: (0,) * len(shape))
    pick = lambda shape: pl.BlockSpec((None,) + shape, lambda i: (0,) * (len(shape) + 1))
    side = rows // 2 + 8
    outs = [(rows + 8, jnp.float32)] * 2 + [(side, jnp.float32)] * 2 + [(cols // 2, jnp.bfloat16)] * 2
    left1, right1, left2, right2, top2, bot2 = pl.pallas_call(
        rim_body,
        grid=(1,),
        in_specs=[pl.BlockSpec(memory_space=pltpu.SMEM)]
        + [whole(sides[0].shape)] * 4
        + [whole(top.shape)] * 2
        + [
            pl.BlockSpec((1, cols, channels), lambda i: (0, 0, 0)),
            pl.BlockSpec((1, cols, channels), lambda i: (rows - 1, 0, 0)),
            pick((16, channels)),
            pick((1, channels)),
            pick((channels, hid)),
            pick((hid, channels)),
        ],
        out_specs=[whole((count, channels)) for count, _ in outs],
        out_shape=[jax.ShapeDtypeStruct((count, channels), kind) for count, kind in outs],
        scratch_shapes=[
            pltpu.VMEM((8, 2, rows + 4 * PAD, 128), jnp.float32),
            pltpu.VMEM((8, 2, cols + 2 * PAD, 128), jnp.float32),
            pltpu.VMEM((2 * side + cols, channels), jnp.float32),
        ],
        compiler_params=pltpu.CompilerParams(vmem_limit_bytes=20 << 20),
        name="rim",
    )(edge, from_left, from_right, *sides, top, bot, far(current), far(current), dw_kernel,
      norm_gain[:, None, :], far(w_in), far(w_out))
    return (top[-1], bot[0], left1, right1), (top2, bot2, left2, right2)


def run_layer(current, halo, layer, dw_kernel, norm_gain, w_in, w_out, w_flux, rows, late=()):
    in_rows, in_cols, channels = current.shape
    out_rows, out_cols = in_rows // 2, in_cols // 2
    hid = w_in.shape[2]
    steps = out_rows // rows
    with_flux = w_flux is not None
    whole = lambda shape: pl.BlockSpec(shape, lambda i: (0,) * len(shape))
    pick = lambda shape: pl.BlockSpec((None,) + shape, lambda i: (layer,) + (0,) * len(shape))
    in_specs = [
        pl.BlockSpec((2 * rows, in_cols, channels), lambda i: (i, 0, 0)),
        pl.BlockSpec((1, in_cols, channels), lambda i: (jnp.maximum(2 * rows * i - 1, 0), 0, 0)),
        pl.BlockSpec(
            (1, in_cols, channels), lambda i: (jnp.minimum(2 * rows * (i + 1), in_rows - 1), 0, 0)
        ),
        whole((in_cols, channels)),
        whole((in_cols, channels)),
        whole((in_rows + 8, channels)),
        whole((in_rows + 8, channels)),
        pick((16, channels)),
        pick((1, channels)),
        pick((channels, hid)),
        pick((hid, channels)),
    ]
    field = current if with_flux else far(current)
    operands = [field, field, field, *halo, dw_kernel, norm_gain[:, None, :], far(w_in), far(w_out)]
    cells = out_rows * out_cols
    if with_flux:
        table, weights = late
        in_specs += [
            whole((channels, channels)),
            pl.BlockSpec(memory_space=pltpu.SMEM),
            pl.BlockSpec(memory_space=pl.ANY),
        ]
        operands += [w_flux, table, far(weights)]
        _, ocean, tile = weights.shape
        out_specs = [
            pl.BlockSpec((rows * out_cols, channels), lambda i: (i, 0)),
            whole((ocean, OWNERS, channels)),
        ]
        out_shape = [
            jax.ShapeDtypeStruct((cells, channels), jnp.bfloat16),
            jax.ShapeDtypeStruct((ocean, OWNERS, channels), jnp.bfloat16),
        ]
        extra = [
            pltpu.VMEM((cells, channels), jnp.bfloat16),
            pltpu.VMEM((OWNERS, ocean, tile), jnp.bfloat16),
            pltpu.VMEM((2, OWNERS * ocean, 128), jnp.float32),
            pltpu.SemaphoreType.DMA((OWNERS,)),
        ]
    else:
        extra = []
        out_specs = pl.BlockSpec((rows, out_cols, channels), lambda i: (i, 0, 0))
        out_shape = jax.ShapeDtypeStruct((out_rows, out_cols, channels), jnp.bfloat16)

    def body(*refs):
        if with_flux:
            layer_body(rows, in_cols, steps, True, *refs)
        else:
            layer_body(rows, in_cols, steps, False, *refs[:12], None, *refs[12:])

    return pl.pallas_call(
        body,
        grid=(steps,),
        in_specs=in_specs,
        out_specs=out_specs,
        out_shape=out_shape,
        scratch_shapes=[
            pltpu.VMEM((2 * rows + 2, 2, in_cols + 2 * PAD, 128), jnp.float32),
            pltpu.VMEM((rows * out_cols, channels), jnp.float32),
        ] + extra,
        compiler_params=pltpu.CompilerParams(vmem_limit_bytes=28 << 20),
        cost_estimate=pl.CostEstimate(
            flops=cells * channels * hid // 4, transcendentals=0,
            bytes_accessed=2 * (in_rows * in_cols + cells) * channels,
        ),
        name="layer",
    )(*operands)


def index(shape, dim):
    return lax.broadcasted_iota(jnp.int32, shape, dim)


def matmul(lhs, rhs, rhs_dim):
    return lax.dot_general(
        lhs.astype(jnp.float32), rhs.astype(jnp.float32), (((1,), (rhs_dim,)), ((), ())),
        preferred_element_type=jnp.float32,
    )


def column_of(row):
    size = row.shape[1]
    square = (size, size)
    diagonal = index(square, 0) == index(square, 1)
    return jnp.sum(jnp.where(diagonal, jnp.broadcast_to(row, square), 0), axis=1, keepdims=True)


def route_body(owner_ref, ocean_ref, tile_ref, out_ref, code_ref):
    owner_row = owner_ref[...]
    blocks = owner_row.shape[1]
    owner, ocean, tile = (column_of(ref[...]) for ref in (owner_ref, ocean_ref, tile_ref))
    square = (blocks, blocks)
    same = (owner == owner_row) & (index(square, 1) < index(square, 0))
    rank = jnp.sum(same.astype(jnp.int32), axis=1, keepdims=True)
    mine = owner == index(square, 1)
    code = jnp.zeros((1, blocks), jnp.int32)
    for r in range(CAP):
        hit = (mine & (rank == r)).astype(jnp.int32)
        sums = lambda column: jnp.sum(hit * column, axis=0, keepdims=True)
        code = code * 32 + sums(ocean + 1)
        out_ref[r:r + 1, :] = sums(index((blocks, 1), 0))
        out_ref[2 + r:3 + r, :] = sums(tile)
    out_ref[4:8, :] = jnp.zeros((4, blocks), jnp.int32)
    code_ref[...] = jnp.broadcast_to(code, code_ref.shape)


def route(owner, ocean, tile):
    blocks = owner.shape[0]
    return pl.pallas_call(
        route_body,
        out_shape=[
            jax.ShapeDtypeStruct((8, blocks), jnp.int32),
            jax.ShapeDtypeStruct((blocks, blocks), jnp.int32),
        ],
        name="route",
    )(owner.reshape(1, blocks), ocean.reshape(1, blocks), tile.reshape(1, blocks))


def plan_body(me_ref, table_ref, own_ref, row_ref, bins_ref):
    code = table_ref[...]
    devices = code.shape[0]
    square = (devices, devices)
    spare = code & 31
    hot = jnp.max(spare, axis=0, keepdims=True) > 0
    hot8 = jnp.broadcast_to(hot, (8, devices)).astype(jnp.float32)
    before = (index(square, 0) < index(square, 1)).astype(jnp.float32)
    rank = matmul(hot8, before, 0).astype(jnp.int32)
    listed = (jnp.broadcast_to(hot, square) & (rank[:1] == index(square, 0))).astype(jnp.float32)
    bins_ref[...] = matmul(listed, spare, 1).astype(jnp.int32) - 1
    me = (index((8, devices), 1) == me_ref[0]).astype(jnp.float32)
    row_ref[0:8] = matmul(me, code >> 5, 1).astype(jnp.int32) - 1
    row_ref[8:16] = matmul(own_ref[...], listed, 1).astype(jnp.int32)
    row_ref[16:24] = jnp.where(hot8 > 0, rank, -1)
    row_ref[24:32] = jnp.broadcast_to(
        jnp.sum(hot8, axis=1, keepdims=True).astype(jnp.int32), (8, devices)
    )


def plan(me, table, own):
    devices = table.shape[0]
    vmem = pl.BlockSpec(memory_space=pltpu.VMEM)
    return pl.pallas_call(
        plan_body,
        in_specs=[pl.BlockSpec(memory_space=pltpu.SMEM), vmem, vmem],
        out_specs=[vmem, vmem],
        out_shape=[
            jax.ShapeDtypeStruct((32, devices), jnp.int32),
            jax.ShapeDtypeStruct((devices, devices), jnp.int32),
        ],
        name="plan",
    )(me.reshape(1), table, own)


def spare_copies(first, row_ref, w_ref, weights, sems):
    return [
        pltpu.make_async_copy(w_ref.at[row_ref[9, first + h]], weights.at[h], sems.at[h])
        for h in range(OWNERS)
    ]


def spare_rows(first, row_ref, weights, tile_of, out_ref, spare):
    cells = weights.shape[1]
    for h in range(OWNERS):
        rows = slice(h * cells, h * cells + cells)
        value = jnp.dot(
            weights[h], tile_of(row_ref[11, first + h]), preferred_element_type=jnp.float32
        )
        spare[0, rows, :] = value[:, :128]
        spare[1, rows, :] = value[:, 128:]
    for half in range(2):
        lanes = slice(128 * half, 128 * half + 128)
        for g in range(0, cells, 32):
            block = spare[half].reshape(OWNERS, cells, 128)[:, g:g + 32, :]
            out_ref[g:g + 32, :, lanes] = jnp.swapaxes(block, 0, 1).astype(jnp.bfloat16)


def spare_body(turn_ref, row_ref, w_ref, flux_ref, out_ref, weights, spare, sems):
    first = turn_ref[0] * OWNERS
    copies = spare_copies(first, row_ref, w_ref, weights, sems)
    for copy in copies:
        copy.start()
    for copy in copies:
        copy.wait()
    spare_rows(first, row_ref, weights, lambda tile: flux_ref[tile], out_ref, spare)


def remap_spare(turn, rows, weights, flux):
    _, cells, tile = weights.shape
    channels = flux.shape[2]
    out = (cells, OWNERS, channels)
    grid_spec = pltpu.PrefetchScalarGridSpec(
        num_scalar_prefetch=2,
        grid=(1,),
        in_specs=[
            pl.BlockSpec(memory_space=pl.ANY),
            pl.BlockSpec(flux.shape, lambda i, *_: (0, 0, 0)),
        ],
        out_specs=pl.BlockSpec(out, lambda i, *_: (0, 0, 0)),
        scratch_shapes=[
            pltpu.VMEM((OWNERS, cells, tile), jnp.bfloat16),
            pltpu.VMEM((2, OWNERS * cells, 128), jnp.float32),
            pltpu.SemaphoreType.DMA((OWNERS,)),
        ],
    )
    return pl.pallas_call(
        spare_body,
        grid_spec=grid_spec,
        out_shape=jax.ShapeDtypeStruct(out, jnp.bfloat16),
        compiler_params=pltpu.CompilerParams(vmem_limit_bytes=16 << 20),
        name="remap_spare",
    )(turn.reshape(1), rows, far(weights), flux)


def remap_body(group, own_ref, w_ref, flux_ref, out_ref):
    base = pl.program_id(0) * group
    for j in range(group):
        out_ref[j] = jnp.dot(
            w_ref[own_ref[0, base + j]], flux_ref[own_ref[2, base + j]],
            preferred_element_type=jnp.float32,
        ).astype(jnp.bfloat16)


def remap(own, weights, flux):
    group = 16
    devices, cells, tile = weights.shape
    channels = flux.shape[2]
    grid_spec = pltpu.PrefetchScalarGridSpec(
        num_scalar_prefetch=1,
        grid=(devices // group,),
        in_specs=[
            pl.BlockSpec(weights.shape, lambda i, *_: (0, 0, 0)),
            pl.BlockSpec(flux.shape, lambda i, *_: (0, 0, 0)),
        ],
        out_specs=pl.BlockSpec((group, cells, channels), lambda i, *_: (i, 0, 0)),
    )
    return pl.pallas_call(
        functools.partial(remap_body, group),
        grid_spec=grid_spec,
        out_shape=pltpu.HBM((devices, cells + OB_DEV, channels), jnp.bfloat16),
        compiler_params=pltpu.CompilerParams(vmem_limit_bytes=56 << 20),
        name="remap",
    )(own, far(weights), flux)


def spread(x_ref, flat):
    count, rows, _ = x_ref.shape

    def fill(s, carry):
        start = pl.multiple_of(s * rows, rows)
        value = x_ref[s].astype(jnp.float32)
        flat[0, pl.ds(start, rows), :] = value[:, :128]
        flat[1, pl.ds(start, rows), :] = value[:, 128:]
        return carry

    lax.fori_loop(0, count, fill, 0, unroll=8)


def part_body(turn_ref, row_ref, bins_ref, x_ref, *refs):
    out_ref, flat, sums = refs[-3:]
    sources, rows, _ = x_ref.shape
    spread(x_ref, flat)
    for h in range(rows):
        spot = jnp.broadcast_to(bins_ref[h:h + 1, :], (OB_DEV, sources))
        chosen = (spot == index((OB_DEV, sources), 0)).astype(jnp.bfloat16)
        for half in range(2):
            value = flat[half, pl.ds(h, sources, stride=rows), :].astype(jnp.bfloat16)
            sums[h, :, 128 * half:128 * half + 128] = jnp.dot(
                chosen, value, preferred_element_type=jnp.float32
            ).astype(jnp.bfloat16)

    def deal(d, carry):
        rank = row_ref[16, d] - turn_ref[0] * OWNERS
        out_ref[d] = sums[jnp.clip(rank, 0, OWNERS - 1)]
        return carry

    lax.fori_loop(0, out_ref.shape[0], deal, 0, unroll=8)


def part_sum(turn, rows, bins, arrived, slots):
    devices, _, channels = arrived.shape
    in_specs = [
        pl.BlockSpec((OWNERS, devices), lambda i, turn, _: (turn[0], 0)),
        pl.BlockSpec((devices, OWNERS, channels), lambda i, *_: (0, 0, 0)),
    ]
    operands = [turn.reshape(1), rows, bins, arrived]
    tail, aliases = 0, {}
    out_shape = jax.ShapeDtypeStruct((devices, OB_DEV, channels), jnp.bfloat16)
    if slots is not None:
        in_specs.append(pl.BlockSpec(memory_space=pl.ANY))
        operands.append(slots)
        tail, aliases = slots.shape[1] // OB_DEV - 1, {4: 0}
        out_shape = pltpu.HBM(slots.shape, jnp.bfloat16)
    grid_spec = pltpu.PrefetchScalarGridSpec(
        num_scalar_prefetch=2,
        grid=(1,),
        in_specs=in_specs,
        out_specs=pl.BlockSpec((devices, OB_DEV, channels), lambda i, *_: (0, tail, 0)),
        scratch_shapes=[
            pltpu.VMEM((2, devices * OWNERS, 128), jnp.float32),
            pltpu.VMEM((OWNERS, OB_DEV, channels), jnp.bfloat16),
        ],
    )
    return pl.pallas_call(
        part_body,
        grid_spec=grid_spec,
        out_shape=out_shape,
        input_output_aliases=aliases,
        compiler_params=pltpu.CompilerParams(vmem_limit_bytes=14 << 20),
        name="part_sum",
    )(*operands)


def owner_body(group, me_ref, row_ref, x_ref, out_ref, total, flat):
    step = pl.program_id(0)
    rows = OB_DEV
    cells = out_ref.shape[1]
    devices = pl.num_programs(0) * group
    rank = row_ref[16, me_ref[0]]
    served = (rank >= 0) & (rank < OWNERS)

    @pl.when(step == 0)
    def _():
        total[...] = jnp.zeros_like(total)

    for j in range(group):
        source = step * group + j
        spot = row_ref[0, source]
        spot = jnp.where(spot < 0, OB_DEV, spot)
        total[spot] += x_ref[j, :cells, :].astype(jnp.float32)
        start = pl.multiple_of(source * rows, rows)
        value = x_ref[j, cells:, :].astype(jnp.float32)
        flat[0, pl.ds(start, rows), :] = value[:, :128]
        flat[1, pl.ds(start, rows), :] = value[:, 128:]

    last = step == pl.num_programs(0) - 1

    @pl.when(last & jnp.logical_not(served))
    def _():
        out_ref[...] = total[:OB_DEV]

    @pl.when(last & served)
    def _():
        for b in range(OB_DEV):
            for half in range(2):
                lanes = slice(128 * half, 128 * half + 128)
                late = flat[half, pl.ds(b, cells, stride=rows), :]
                out_ref[b, :, lanes] = total[b, :, lanes] + late


def owner_sum(me, rows, arrived, group):
    devices, both, channels = arrived.shape
    cells = both - OB_DEV
    grid_spec = pltpu.PrefetchScalarGridSpec(
        num_scalar_prefetch=2,
        grid=(devices // group,),
        in_specs=[pl.BlockSpec((group, both, channels), lambda i, *_: (i, 0, 0))],
        out_specs=pl.BlockSpec((OB_DEV, cells, channels), lambda i, *_: (0, 0, 0)),
        scratch_shapes=[
            pltpu.VMEM((OB_DEV + 1, cells, channels), jnp.float32),
            pltpu.VMEM((2, devices * OB_DEV, 128), jnp.float32),
        ],
    )
    return pl.pallas_call(
        functools.partial(owner_body, group),
        grid_spec=grid_spec,
        out_shape=jax.ShapeDtypeStruct((OB_DEV, cells, channels), jnp.float32),
        compiler_params=pltpu.CompilerParams(vmem_limit_bytes=24 << 20),
        name="owner_sum",
    )(me.reshape(1), rows, arrived)


def late_body(rank_ref, total_ref, x_ref, out_ref, flat):
    rows = x_ref.shape[1]
    devices = x_ref.shape[0]
    out_ref[...] = total_ref[...]

    @pl.when((rank_ref[0] >= 0) & (rank_ref[0] < OWNERS))
    def _():
        spread(x_ref, flat)
        for b in range(rows):
            for half in range(2):
                lanes = slice(128 * half, 128 * half + 128)
                out_ref[b, :, lanes] += flat[half, pl.ds(b, devices, stride=rows), :]


def late_sum(rank, total, arrived):
    vmem = pl.BlockSpec(memory_space=pltpu.VMEM)
    return pl.pallas_call(
        late_body,
        in_specs=[pl.BlockSpec(memory_space=pltpu.SMEM), vmem, vmem],
        out_specs=vmem,
        out_shape=jax.ShapeDtypeStruct(total.shape, jnp.float32),
        scratch_shapes=[pltpu.VMEM((2, arrived.shape[0] * OB_DEV, 128), jnp.float32)],
        compiler_params=pltpu.CompilerParams(vmem_limit_bytes=14 << 20),
        name="late_sum",
    )(rank.reshape(1), total, arrived)


def exchange(value):
    return lax.all_to_all(value, BOTH, split_axis=0, concat_axis=0, tiled=True)


def shards(atmosphere, dw_kernel, norm_gain, w_in, w_out, w_flux, remap_weight, block_tile,
           block_owner, block_ocean):
    devices = lax.axis_size("lat") * lax.axis_size("lon")
    cells = remap_weight.shape[1]
    assert devices == cells == block_tile.shape[0]
    me = lax.axis_index(BOTH)
    own, code = route(block_owner, block_ocean, block_tile)
    table = exchange(code)
    mixer = (dw_kernel, norm_gain, w_in, w_out)
    rim1, rim2 = rims(atmosphere, *mixer)
    hidden = run_layer(atmosphere, rim1, 0, *mixer, None, 32)
    hidden, table = lax.optimization_barrier((hidden, table))
    rows, bins = plan(me, table, own)
    flux, spare = run_layer(hidden, rim2, 1, *mixer, w_flux, 32, (rows, remap_weight))
    channels = flux.shape[1]
    flux = flux.reshape(-1, remap_weight.shape[2], channels)
    first = jnp.int32(0)
    count = rows[24, 0]
    parts = exchange(spare)
    sending = part_sum(first, rows, bins, parts, remap(own, remap_weight, flux))
    total = owner_sum(me, rows, exchange(sending), 16)

    def more(state):
        return state[0] * OWNERS < count

    def again(state):
        turn, total = state
        parts = exchange(remap_spare(turn, rows, remap_weight, flux))
        late = exchange(part_sum(turn, rows, bins, parts, None))
        rank = lax.dynamic_index_in_dim(rows[16], me, keepdims=False)
        return turn + 1, late_sum(rank - turn * OWNERS, total, late)

    _, total = lax.while_loop(more, again, (first + 1, total))
    return total.reshape(-1, channels)


def solution(mesh):
    placed = (
        P("lat", "lon", None),
        P(),
        P(),
        P(),
        P(),
        P(),
        P(BOTH, None, None),
        P(BOTH),
        P(BOTH, None),
        P(BOTH),
    )
    return jax.shard_map(
        shards, mesh=mesh, in_specs=placed, out_specs=P(BOTH, None), check_vma=False
    )
```

```python
import functools
import jax
import jax.numpy as jnp
from jax import lax
from jax.experimental import pallas as pl
from jax.experimental.pallas import tpu as pltpu
from jax.sharding import PartitionSpec as P

CAP = 2
OB_DEV = 16
OWNERS = 16


def far(value):
    return pltpu.with_memory_space_constraint(value, pltpu.HBM)

BOTH = ("lat", "lon")
PAD = 8
GELU_A = 0.7978845608028654
GELU_B = 0.044715 * GELU_A


def shift(value, axis, periodic):
    count = lax.axis_size(axis)
    forward = [(i, i + 1) for i in range(count - 1)]
    if periodic:
        forward.append((count - 1, 0))
    backward = [(target, source) for source, target in forward]
    return (
        lax.ppermute(value[1], axis, forward),
        lax.ppermute(value[0], axis, backward),
    )


def mix(depth, gain, win_ref, wout_ref):
    flat = depth.astype(jnp.bfloat16).astype(jnp.float32)
    mean_sq = jnp.mean(flat * flat, axis=-1, keepdims=True)
    normed = (flat * lax.rsqrt(mean_sq + 1e-06) * gain).astype(jnp.bfloat16)
    wide = jnp.dot(normed, win_ref[...], preferred_element_type=jnp.float32)
    inner = wide * (GELU_A + GELU_B * (wide * wide))
    hidden = (wide * (0.5 + 0.5 * jnp.tanh(inner))).astype(jnp.bfloat16)
    return flat + jnp.dot(hidden, wout_ref[...], preferred_element_type=jnp.float32)


def layer_body(rows, cols, steps, with_flux, *refs):
    if with_flux:
        (x_ref, prev_ref, next_ref, top_ref, bot_ref, left_ref, right_ref, kern_ref, gain_ref,
         win_ref, wout_ref, wflux_ref, row_ref, remap_ref, out_ref, spare_ref, xs, dep, flux, weights,
         spare, sems) = refs
    else:
        (x_ref, prev_ref, next_ref, top_ref, bot_ref, left_ref, right_ref, kern_ref, gain_ref,
         win_ref, wout_ref, out_ref, edge_ref, xs, dep) = refs
    step = pl.program_id(0)
    half = cols // 2
    if with_flux:
        copies = spare_copies(0, row_ref, remap_ref, weights, sems)

        @pl.when(step == 0)
        def _():
            for copy in copies:
                copy.start()

    def put(slot, value):
        value = value.astype(jnp.float32)
        xs[slot, 0, PAD:PAD + cols, :] = value[:, :128]
        xs[slot, 1, PAD:PAD + cols, :] = value[:, 128:]

    first = jnp.where(step == 0, top_ref[...].astype(jnp.float32), prev_ref[0].astype(jnp.float32))
    last = jnp.where(
        step == steps - 1, bot_ref[...].astype(jnp.float32), next_ref[0].astype(jnp.float32)
    )
    put(0, first)
    put(2 * rows + 1, last)
    for r in range(2 * rows):
        put(r + 1, x_ref[r])
    base = pl.multiple_of(step * (2 * rows), 2 * rows)
    near = left_ref[pl.ds(base, 2 * rows + 8), :]
    after = right_ref[pl.ds(base, 2 * rows + 8), :]
    for r in range(2 * rows + 2):
        for h in range(2):
            lanes = slice(128 * h, 128 * h + 128)
            xs[r, h, PAD - 1:PAD, :] = near[r:r + 1, lanes]
            xs[r, h, PAD + cols:PAD + cols + 1, :] = after[r:r + 1, lanes]
    for h in range(2):
        lanes = slice(128 * h, 128 * h + 128)
        for k in range(rows):
            total = jnp.zeros((half, 128), jnp.float32)
            for p in range(4):
                for q in range(4):
                    window = xs[2 * k + p, h, pl.ds(PAD - 1 + q, half, stride=2), :]
                    total = total + window * kern_ref[4 * p + q:4 * p + q + 1, lanes]
            dep[k * half:(k + 1) * half, lanes] = total
    layer = int(with_flux)
    mixed = mix(dep[...], gain_ref[layer:layer + 1, :], win_ref, wout_ref)
    if with_flux:
        value = jnp.dot(
            mixed.astype(jnp.bfloat16), wflux_ref[...], preferred_element_type=jnp.float32
        ).astype(jnp.bfloat16)
        out_ref[...] = value
        count = rows * half
        flux[pl.ds(pl.multiple_of(step * count, count), count), :] = value
        cells = weights.shape[2]

        @pl.when(step == steps - 1)
        def _():
            for copy in copies:
                copy.wait()
            tile_of = lambda tile: flux[pl.ds(pl.multiple_of(tile * cells, cells), cells), :]
            spare_rows(0, row_ref, weights, tile_of, spare_ref, spare)

    else:
        out_ref[...] = mixed.astype(jnp.bfloat16).reshape(rows, half, mixed.shape[1])


def rim_body(edge_ref, from_left, from_right, left_ref, right_ref, top_ref, bot_ref, first_ref,
             last_ref, kern_ref, gain_ref, win_ref, wout_ref, left1, right1, left2, right2, top2,
             bot2, tall, wide, cells):
    rows = left_ref.shape[1] - 16
    cols = first_ref.shape[1]
    half_cols = cols // 2
    side = left2.shape[0]
    halves = [(h, slice(128 * h, 128 * h + 128)) for h in range(2)]
    strips = [(from_left, c) for c in range(3)] + [(left_ref, 0)]
    strips += [(right_ref, 2)] + [(from_right, c) for c in range(3)]
    for n, (ref, c) in enumerate(strips):
        value = ref[c].astype(jnp.float32)
        for h, lanes in halves:
            tall[n, h, PAD:PAD + rows, :] = value[:rows, lanes]
            tall[n, h, PAD - 3:PAD, :] = value[rows:rows + 3, lanes]
            tall[n, h, PAD + rows:PAD + rows + 3, :] = value[rows + 3:rows + 6, lanes]
            tall[n, h, PAD + rows + 3:, :] = jnp.zeros(
                (tall.shape[2] - PAD - rows - 3, 128), jnp.float32
            )
    for h, lanes in halves:
        left1[:, lanes] = tall[2, h, PAD - 1:PAD - 1 + left1.shape[0], :]
        right1[:, lanes] = tall[5, h, PAD - 1:PAD - 1 + right1.shape[0], :]
    lines = [(top_ref[i], i - 3) for i in range(3)] + [(first_ref[0], 0)]
    lines += [(last_ref[0], rows - 1)] + [(bot_ref[i], rows + i) for i in range(3)]
    for n, (value, row) in enumerate(lines):
        value = value.astype(jnp.float32)
        at = PAD + row
        for h, lanes in halves:
            wide[n, h, PAD:PAD + cols, :] = value[:, lanes]
            wide[n, h, PAD - 1:PAD, :] = tall[2, h, at:at + 1, :]
            wide[n, h, PAD + cols:PAD + cols + 1, :] = tall[5, h, at:at + 1, :]
    for h, lanes in halves:
        for part in range(2):
            total = jnp.zeros((side, 128), jnp.float32)
            line = jnp.zeros((half_cols, 128), jnp.float32)
            for p in range(4):
                for q in range(4):
                    tap = kern_ref[4 * p + q:4 * p + q + 1, lanes]
                    total = total + tall[4 * part + q, h, pl.ds(PAD - 3 + p, side, stride=2), :] * tap
                    line = line + wide[4 * part + p, h, pl.ds(PAD - 1 + q, half_cols, stride=2), :] * tap
            cells[side * part:side * part + side, lanes] = total
            at = 2 * side + half_cols * part
            cells[at:at + half_cols, lanes] = line
    mixed = mix(cells[...], gain_ref[:1, :], win_ref, wout_ref).astype(jnp.bfloat16).astype(jnp.float32)
    place = index((side, mixed.shape[1]), 0)
    outside = ((place == 0) & (edge_ref[0] > 0)) | ((place == rows // 2 + 1) & (edge_ref[1] > 0))
    left2[...] = jnp.where(outside, 0.0, mixed[:side])
    right2[...] = jnp.where(outside, 0.0, mixed[side:2 * side])
    at = 2 * side
    top2[...] = jnp.where(edge_ref[0] > 0, 0.0, mixed[at:at + half_cols]).astype(jnp.bfloat16)
    bot2[...] = jnp.where(edge_ref[1] > 0, 0.0, mixed[at + half_cols:]).astype(jnp.bfloat16)


def rims(current, dw_kernel, norm_gain, w_in, w_out):
    rows, cols, channels = current.shape
    hid = w_in.shape[2]
    top, bot = shift((current[:3], current[-3:]), "lat", False)
    fill = jnp.zeros((3, 10, channels), current.dtype)
    sides = [
        jnp.concatenate(
            [jnp.swapaxes(part[:, c:c + 3], 0, 1) for part in (current, top, bot)] + [fill], axis=1
        )
        for c in (0, cols - 3)
    ]
    from_left, from_right = shift(sides, "lon", True)
    lat = lax.axis_index("lat")
    edge = jnp.stack([lat == 0, lat == lax.axis_size("lat") - 1]).astype(jnp.int32)
    whole = lambda shape: pl.BlockSpec(shape, lambda i: (0,) * len(shape))
    pick = lambda shape: pl.BlockSpec((None,) + shape, lambda i: (0,) * (len(shape) + 1))
    side = rows // 2 + 8
    outs = [(rows + 8, jnp.float32)] * 2 + [(side, jnp.float32)] * 2 + [(cols // 2, jnp.bfloat16)] * 2
    left1, right1, left2, right2, top2, bot2 = pl.pallas_call(
        rim_body,
        grid=(1,),
        in_specs=[pl.BlockSpec(memory_space=pltpu.SMEM)]
        + [whole(sides[0].shape)] * 4
        + [whole(top.shape)] * 2
        + [
            pl.BlockSpec((1, cols, channels), lambda i: (0, 0, 0)),
            pl.BlockSpec((1, cols, channels), lambda i: (rows - 1, 0, 0)),
            pick((16, channels)),
            whole(norm_gain.shape),
            pick((channels, hid)),
            pick((hid, channels)),
        ],
        out_specs=[whole((count, channels)) for count, _ in outs],
        out_shape=[jax.ShapeDtypeStruct((count, channels), kind) for count, kind in outs],
        scratch_shapes=[
            pltpu.VMEM((8, 2, rows + 4 * PAD, 128), jnp.float32),
            pltpu.VMEM((8, 2, cols + 2 * PAD, 128), jnp.float32),
            pltpu.VMEM((2 * side + cols, channels), jnp.float32),
        ],
        compiler_params=pltpu.CompilerParams(vmem_limit_bytes=20 << 20),
        name="rim",
    )(edge, from_left, from_right, *sides, top, bot, far(current), far(current), dw_kernel,
      norm_gain, far(w_in), far(w_out))
    return (top[-1], bot[0], left1, right1), (top2, bot2, left2, right2)


def run_layer(current, halo, layer, dw_kernel, norm_gain, w_in, w_out, w_flux, rows, late=()):
    in_rows, in_cols, channels = current.shape
    out_rows, out_cols = in_rows // 2, in_cols // 2
    hid = w_in.shape[2]
    steps = out_rows // rows
    with_flux = w_flux is not None
    whole = lambda shape: pl.BlockSpec(shape, lambda i: (0,) * len(shape))
    pick = lambda shape: pl.BlockSpec((None,) + shape, lambda i: (layer,) + (0,) * len(shape))
    in_specs = [
        pl.BlockSpec((2 * rows, in_cols, channels), lambda i: (i, 0, 0)),
        pl.BlockSpec((1, in_cols, channels), lambda i: (jnp.maximum(2 * rows * i - 1, 0), 0, 0)),
        pl.BlockSpec(
            (1, in_cols, channels), lambda i: (jnp.minimum(2 * rows * (i + 1), in_rows - 1), 0, 0)
        ),
        whole((in_cols, channels)),
        whole((in_cols, channels)),
        whole((in_rows + 8, channels)),
        whole((in_rows + 8, channels)),
        pick((16, channels)),
        whole(norm_gain.shape),
        pick((channels, hid)),
        pick((hid, channels)),
    ]
    field = current if with_flux else far(current)
    operands = [field, field, field, *halo, dw_kernel, norm_gain, far(w_in), far(w_out)]
    cells = out_rows * out_cols
    if with_flux:
        table, weights = late
        in_specs += [
            whole((channels, channels)),
            pl.BlockSpec(memory_space=pltpu.SMEM),
            pl.BlockSpec(memory_space=pl.ANY),
        ]
        operands += [w_flux, table, far(weights)]
        _, ocean, tile = weights.shape
        out_specs = [
            pl.BlockSpec((rows * out_cols, channels), lambda i: (i, 0)),
            whole((ocean, OWNERS, channels)),
        ]
        out_shape = [
            jax.ShapeDtypeStruct((cells, channels), jnp.bfloat16),
            jax.ShapeDtypeStruct((ocean, OWNERS, channels), jnp.bfloat16),
        ]
        extra = [
            pltpu.VMEM((cells, channels), jnp.bfloat16),
            pltpu.VMEM((OWNERS, ocean, tile), jnp.bfloat16),
            pltpu.VMEM((2, OWNERS * ocean, 128), jnp.float32),
            pltpu.SemaphoreType.DMA((OWNERS,)),
        ]
    else:
        extra = []
        out_specs = pl.BlockSpec((rows, out_cols, channels), lambda i: (i, 0, 0))
        out_shape = jax.ShapeDtypeStruct((out_rows, out_cols, channels), jnp.bfloat16)

    def body(*refs):
        if with_flux:
            layer_body(rows, in_cols, steps, True, *refs)
        else:
            layer_body(rows, in_cols, steps, False, *refs[:12], None, *refs[12:])

    return pl.pallas_call(
        body,
        grid=(steps,),
        in_specs=in_specs,
        out_specs=out_specs,
        out_shape=out_shape,
        scratch_shapes=[
            pltpu.VMEM((2 * rows + 2, 2, in_cols + 2 * PAD, 128), jnp.float32),
            pltpu.VMEM((rows * out_cols, channels), jnp.float32),
        ] + extra,
        compiler_params=pltpu.CompilerParams(vmem_limit_bytes=28 << 20),
        cost_estimate=pl.CostEstimate(
            flops=cells * channels * hid // 4, transcendentals=0,
            bytes_accessed=2 * (in_rows * in_cols + cells) * channels,
        ),
        name="layer",
    )(*operands)


def index(shape, dim):
    return lax.broadcasted_iota(jnp.int32, shape, dim)


def matmul(lhs, rhs, rhs_dim):
    return lax.dot_general(
        lhs.astype(jnp.float32), rhs.astype(jnp.float32), (((1,), (rhs_dim,)), ((), ())),
        preferred_element_type=jnp.float32,
    )


def column_of(row):
    size = row.shape[1]
    square = (size, size)
    diagonal = index(square, 0) == index(square, 1)
    return jnp.sum(jnp.where(diagonal, jnp.broadcast_to(row, square), 0), axis=1, keepdims=True)


def route_body(owner_ref, ocean_ref, tile_ref, out_ref, code_ref):
    owner_row = owner_ref[...]
    blocks = owner_row.shape[1]
    owner, ocean, tile = (column_of(ref[...]) for ref in (owner_ref, ocean_ref, tile_ref))
    square = (blocks, blocks)
    same = (owner == owner_row) & (index(square, 1) < index(square, 0))
    rank = jnp.sum(same.astype(jnp.int32), axis=1, keepdims=True)
    mine = owner == index(square, 1)
    code = jnp.zeros((1, blocks), jnp.int32)
    for r in range(CAP):
        hit = (mine & (rank == r)).astype(jnp.int32)
        sums = lambda column: jnp.sum(hit * column, axis=0, keepdims=True)
        code = code * 32 + sums(ocean + 1)
        out_ref[r:r + 1, :] = sums(index((blocks, 1), 0))
        out_ref[2 + r:3 + r, :] = sums(tile)
    out_ref[4:8, :] = jnp.zeros((4, blocks), jnp.int32)
    code_ref[...] = jnp.broadcast_to(code, code_ref.shape)


def route(owner, ocean, tile):
    blocks = owner.shape[0]
    return pl.pallas_call(
        route_body,
        out_shape=[
            jax.ShapeDtypeStruct((8, blocks), jnp.int32),
            jax.ShapeDtypeStruct((blocks, blocks), jnp.int32),
        ],
        name="route",
    )(owner.reshape(1, blocks), ocean.reshape(1, blocks), tile.reshape(1, blocks))


def plan_body(me_ref, table_ref, own_ref, row_ref, bins_ref):
    code = table_ref[...]
    devices = code.shape[0]
    square = (devices, devices)
    spare = code & 31
    hot = jnp.max(spare, axis=0, keepdims=True) > 0
    hot8 = jnp.broadcast_to(hot, (8, devices)).astype(jnp.float32)
    before = (index(square, 0) < index(square, 1)).astype(jnp.float32)
    rank = matmul(hot8, before, 0).astype(jnp.int32)
    listed = (jnp.broadcast_to(hot, square) & (rank[:1] == index(square, 0))).astype(jnp.float32)
    bins_ref[...] = matmul(listed, spare, 1).astype(jnp.int32) - 1
    me = (index((8, devices), 1) == me_ref[0]).astype(jnp.float32)
    row_ref[0:8] = matmul(me, code >> 5, 1).astype(jnp.int32) - 1
    row_ref[8:16] = matmul(own_ref[...], listed, 1).astype(jnp.int32)
    row_ref[16:24] = jnp.where(hot8 > 0, rank, -1)
    row_ref[24:32] = jnp.broadcast_to(
        jnp.sum(hot8, axis=1, keepdims=True).astype(jnp.int32), (8, devices)
    )


def plan(me, table, own):
    devices = table.shape[0]
    vmem = pl.BlockSpec(memory_space=pltpu.VMEM)
    return pl.pallas_call(
        plan_body,
        in_specs=[pl.BlockSpec(memory_space=pltpu.SMEM), vmem, vmem],
        out_specs=[vmem, vmem],
        out_shape=[
            jax.ShapeDtypeStruct((32, devices), jnp.int32),
            jax.ShapeDtypeStruct((devices, devices), jnp.int32),
        ],
        name="plan",
    )(me.reshape(1), table, own)


def spare_copies(first, row_ref, w_ref, weights, sems):
    return [
        pltpu.make_async_copy(w_ref.at[row_ref[9, first + h]], weights.at[h], sems.at[h])
        for h in range(OWNERS)
    ]


def spare_rows(first, row_ref, weights, tile_of, out_ref, spare):
    cells = weights.shape[1]
    for h in range(OWNERS):
        rows = slice(h * cells, h * cells + cells)
        value = jnp.dot(
            weights[h], tile_of(row_ref[11, first + h]), preferred_element_type=jnp.float32
        )
        spare[0, rows, :] = value[:, :128]
        spare[1, rows, :] = value[:, 128:]
    for half in range(2):
        lanes = slice(128 * half, 128 * half + 128)
        for g in range(0, cells, 32):
            block = spare[half].reshape(OWNERS, cells, 128)[:, g:g + 32, :]
            out_ref[g:g + 32, :, lanes] = jnp.swapaxes(block, 0, 1).astype(jnp.bfloat16)


def spare_body(turn_ref, row_ref, w_ref, flux_ref, out_ref, weights, spare, sems):
    first = turn_ref[0] * OWNERS
    copies = spare_copies(first, row_ref, w_ref, weights, sems)
    for copy in copies:
        copy.start()
    for copy in copies:
        copy.wait()
    spare_rows(first, row_ref, weights, lambda tile: flux_ref[tile], out_ref, spare)


def remap_spare(turn, rows, weights, flux):
    _, cells, tile = weights.shape
    channels = flux.shape[2]
    out = (cells, OWNERS, channels)
    grid_spec = pltpu.PrefetchScalarGridSpec(
        num_scalar_prefetch=2,
        grid=(1,),
        in_specs=[
            pl.BlockSpec(memory_space=pl.ANY),
            pl.BlockSpec(flux.shape, lambda i, *_: (0, 0, 0)),
        ],
        out_specs=pl.BlockSpec(out, lambda i, *_: (0, 0, 0)),
        scratch_shapes=[
            pltpu.VMEM((OWNERS, cells, tile), jnp.bfloat16),
            pltpu.VMEM((2, OWNERS * cells, 128), jnp.float32),
            pltpu.SemaphoreType.DMA((OWNERS,)),
        ],
    )
    return pl.pallas_call(
        spare_body,
        grid_spec=grid_spec,
        out_shape=jax.ShapeDtypeStruct(out, jnp.bfloat16),
        compiler_params=pltpu.CompilerParams(vmem_limit_bytes=16 << 20),
        name="remap_spare",
    )(turn.reshape(1), rows, far(weights), flux)


def remap_body(group, own_ref, w_ref, flux_ref, out_ref):
    base = pl.program_id(0) * group
    for j in range(group):
        out_ref[j] = jnp.dot(
            w_ref[own_ref[0, base + j]], flux_ref[own_ref[2, base + j]],
            preferred_element_type=jnp.float32,
        ).astype(jnp.bfloat16)


def remap(own, weights, flux):
    group = 16
    devices, cells, tile = weights.shape
    channels = flux.shape[2]
    grid_spec = pltpu.PrefetchScalarGridSpec(
        num_scalar_prefetch=1,
        grid=(devices // group,),
        in_specs=[
            pl.BlockSpec(weights.shape, lambda i, *_: (0, 0, 0)),
            pl.BlockSpec(flux.shape, lambda i, *_: (0, 0, 0)),
        ],
        out_specs=pl.BlockSpec((group, cells, channels), lambda i, *_: (i, 0, 0)),
    )
    return pl.pallas_call(
        functools.partial(remap_body, group),
        grid_spec=grid_spec,
        out_shape=pltpu.HBM((devices, cells + OB_DEV, channels), jnp.bfloat16),
        compiler_params=pltpu.CompilerParams(vmem_limit_bytes=56 << 20),
        name="remap",
    )(own, far(weights), flux)


def spread(x_ref, flat):
    count, rows, _ = x_ref.shape

    def fill(s, carry):
        start = pl.multiple_of(s * rows, rows)
        value = x_ref[s].astype(jnp.float32)
        flat[0, pl.ds(start, rows), :] = value[:, :128]
        flat[1, pl.ds(start, rows), :] = value[:, 128:]
        return carry

    lax.fori_loop(0, count, fill, 0, unroll=8)


def part_body(turn_ref, row_ref, bins_ref, x_ref, *refs):
    out_ref, flat, sums = refs[-3:]
    sources, rows, _ = x_ref.shape
    spread(x_ref, flat)
    for h in range(rows):
        spot = jnp.broadcast_to(bins_ref[h:h + 1, :], (OB_DEV, sources))
        chosen = (spot == index((OB_DEV, sources), 0)).astype(jnp.bfloat16)
        for half in range(2):
            value = flat[half, pl.ds(h, sources, stride=rows), :].astype(jnp.bfloat16)
            sums[h, :, 128 * half:128 * half + 128] = jnp.dot(
                chosen, value, preferred_element_type=jnp.float32
            ).astype(jnp.bfloat16)

    def deal(d, carry):
        rank = row_ref[16, d] - turn_ref[0] * OWNERS
        out_ref[d] = sums[jnp.clip(rank, 0, OWNERS - 1)]
        return carry

    lax.fori_loop(0, out_ref.shape[0], deal, 0, unroll=8)


def part_sum(turn, rows, bins, arrived, slots):
    devices, _, channels = arrived.shape
    in_specs = [
        pl.BlockSpec((OWNERS, devices), lambda i, turn, _: (turn[0], 0)),
        pl.BlockSpec((devices, OWNERS, channels), lambda i, *_: (0, 0, 0)),
    ]
    operands = [turn.reshape(1), rows, bins, arrived]
    tail, aliases = 0, {}
    out_shape = jax.ShapeDtypeStruct((devices, OB_DEV, channels), jnp.bfloat16)
    if slots is not None:
        in_specs.append(pl.BlockSpec(memory_space=pl.ANY))
        operands.append(slots)
        tail, aliases = slots.shape[1] // OB_DEV - 1, {4: 0}
        out_shape = pltpu.HBM(slots.shape, jnp.bfloat16)
    grid_spec = pltpu.PrefetchScalarGridSpec(
        num_scalar_prefetch=2,
        grid=(1,),
        in_specs=in_specs,
        out_specs=pl.BlockSpec((devices, OB_DEV, channels), lambda i, *_: (0, tail, 0)),
        scratch_shapes=[
            pltpu.VMEM((2, devices * OWNERS, 128), jnp.float32),
            pltpu.VMEM((OWNERS, OB_DEV, channels), jnp.bfloat16),
        ],
    )
    return pl.pallas_call(
        part_body,
        grid_spec=grid_spec,
        out_shape=out_shape,
        input_output_aliases=aliases,
        compiler_params=pltpu.CompilerParams(vmem_limit_bytes=14 << 20),
        name="part_sum",
    )(*operands)


def owner_body(group, me_ref, row_ref, x_ref, out_ref, total, flat):
    step = pl.program_id(0)
    rows = OB_DEV
    cells = out_ref.shape[1]
    devices = pl.num_programs(0) * group
    rank = row_ref[16, me_ref[0]]
    served = (rank >= 0) & (rank < OWNERS)

    @pl.when(step == 0)
    def _():
        total[...] = jnp.zeros_like(total)

    for j in range(group):
        source = step * group + j
        spot = row_ref[0, source]
        spot = jnp.where(spot < 0, OB_DEV, spot)
        total[spot] += x_ref[j, :cells, :].astype(jnp.float32)
        start = pl.multiple_of(source * rows, rows)
        value = x_ref[j, cells:, :].astype(jnp.float32)
        flat[0, pl.ds(start, rows), :] = value[:, :128]
        flat[1, pl.ds(start, rows), :] = value[:, 128:]

    last = step == pl.num_programs(0) - 1

    @pl.when(last & jnp.logical_not(served))
    def _():
        out_ref[...] = total[:OB_DEV]

    @pl.when(last & served)
    def _():
        for b in range(OB_DEV):
            for half in range(2):
                lanes = slice(128 * half, 128 * half + 128)
                late = flat[half, pl.ds(b, cells, stride=rows), :]
                out_ref[b, :, lanes] = total[b, :, lanes] + late


def owner_sum(me, rows, arrived, group):
    devices, both, channels = arrived.shape
    cells = both - OB_DEV
    grid_spec = pltpu.PrefetchScalarGridSpec(
        num_scalar_prefetch=2,
        grid=(devices // group,),
        in_specs=[pl.BlockSpec((group, both, channels), lambda i, *_: (i, 0, 0))],
        out_specs=pl.BlockSpec((OB_DEV, cells, channels), lambda i, *_: (0, 0, 0)),
        scratch_shapes=[
            pltpu.VMEM((OB_DEV + 1, cells, channels), jnp.float32),
            pltpu.VMEM((2, devices * OB_DEV, 128), jnp.float32),
        ],
    )
    return pl.pallas_call(
        functools.partial(owner_body, group),
        grid_spec=grid_spec,
        out_shape=jax.ShapeDtypeStruct((OB_DEV, cells, channels), jnp.float32),
        compiler_params=pltpu.CompilerParams(vmem_limit_bytes=24 << 20),
        name="owner_sum",
    )(me.reshape(1), rows, arrived)


def late_body(rank_ref, total_ref, x_ref, out_ref, flat):
    rows = x_ref.shape[1]
    devices = x_ref.shape[0]
    out_ref[...] = total_ref[...]

    @pl.when((rank_ref[0] >= 0) & (rank_ref[0] < OWNERS))
    def _():
        spread(x_ref, flat)
        for b in range(rows):
            for half in range(2):
                lanes = slice(128 * half, 128 * half + 128)
                out_ref[b, :, lanes] += flat[half, pl.ds(b, devices, stride=rows), :]


def late_sum(rank, total, arrived):
    vmem = pl.BlockSpec(memory_space=pltpu.VMEM)
    return pl.pallas_call(
        late_body,
        in_specs=[pl.BlockSpec(memory_space=pltpu.SMEM), vmem, vmem],
        out_specs=vmem,
        out_shape=jax.ShapeDtypeStruct(total.shape, jnp.float32),
        scratch_shapes=[pltpu.VMEM((2, arrived.shape[0] * OB_DEV, 128), jnp.float32)],
        compiler_params=pltpu.CompilerParams(vmem_limit_bytes=14 << 20),
        name="late_sum",
    )(rank.reshape(1), total, arrived)


def exchange(value):
    return lax.all_to_all(value, BOTH, split_axis=0, concat_axis=0, tiled=True)


def shards(atmosphere, dw_kernel, norm_gain, w_in, w_out, w_flux, remap_weight, block_tile,
           block_owner, block_ocean):
    devices = lax.axis_size("lat") * lax.axis_size("lon")
    cells = remap_weight.shape[1]
    assert devices == cells == block_tile.shape[0]
    me = lax.axis_index(BOTH)
    own, code = route(block_owner, block_ocean, block_tile)
    table = exchange(code)
    mixer = (dw_kernel, norm_gain, w_in, w_out)
    rim1, rim2 = rims(atmosphere, *mixer)
    hidden = run_layer(atmosphere, rim1, 0, *mixer, None, 32)
    hidden, table = lax.optimization_barrier((hidden, table))
    rows, bins = plan(me, table, own)
    flux, spare = run_layer(hidden, rim2, 1, *mixer, w_flux, 64, (rows, remap_weight))
    channels = flux.shape[1]
    flux = flux.reshape(-1, remap_weight.shape[2], channels)
    first = jnp.int32(0)
    count = rows[24, 0]
    parts = exchange(spare)
    sending = part_sum(first, rows, bins, parts, remap(own, remap_weight, flux))
    total = owner_sum(me, rows, exchange(sending), 16)

    def more(state):
        return state[0] * OWNERS < count

    def again(state):
        turn, total = state
        parts = exchange(remap_spare(turn, rows, remap_weight, flux))
        late = exchange(part_sum(turn, rows, bins, parts, None))
        rank = lax.dynamic_index_in_dim(rows[16], me, keepdims=False)
        return turn + 1, late_sum(rank - turn * OWNERS, total, late)

    _, total = lax.while_loop(more, again, (first + 1, total))
    return total.reshape(-1, channels)


def solution(mesh):
    placed = (
        P("lat", "lon", None),
        P(),
        P(),
        P(),
        P(),
        P(),
        P(BOTH, None, None),
        P(BOTH),
        P(BOTH, None),
        P(BOTH),
    )
    return jax.shard_map(
        shards, mesh=mesh, in_specs=placed, out_specs=P(BOTH, None), check_vma=False
    )
```
